128 devices in a mesh: expert: 16 (over y, x), feat: 8 (over z, core).
Axes of the slice: x: 4, y: 4, z: 4, core: 2. Of those that a mesh axis runs over, the one named last changes fastest.
Arguments:
- tokens: bfloat16 [2048, 2304], P('expert'), may hold values from -6 to 6
- expert_ids: int32 [2048, 8], P(('expert', 'feat')), may hold values from 0 to 127, all different within a row; in each aligned block of 16 rows (0 to 15, 16 to 31, ...) at most 2 rows name the same one
- gate_weights: float32 [2048, 8], P(('expert', 'feat')), may hold values from 0.1 to 0.6
- expert_gate: bfloat16 [128, 2304, 1024], P(('expert', 'feat')), may hold values from -0.125 to 0.125
- expert_up: bfloat16 [128, 2304, 1024], P(('expert', 'feat')), may hold values from -0.125 to 0.125
- expert_down: bfloat16 [128, 1024, 2304], P(('expert', 'feat')), may hold values from -0.1875 to 0.1875
- shared_gate: bfloat16 [2304, 1024], P(None, 'feat'), may hold values from -0.125 to 0.125
- shared_up: bfloat16 [2304, 1024], P(None, 'feat'), may hold values from -0.125 to 0.125
- shared_down: bfloat16 [1024, 2304], P('feat'), may hold values from -0.1875 to 0.1875
- encoder: bfloat16 [2304, 65536], P(None, ('expert', 'feat')), may hold values from -0.125 to 0.125
- encoder_bias: float32 [65536], P(('expert', 'feat')), may hold values from -0.6 to 0.2
- decoder: bfloat16 [65536, 2304], P(('expert', 'feat')), may hold values from -0.0234375 to 0.0234375
- decoder_bias: float32 [2304], replicated, may hold values from -3 to 3
Outputs:
- features: bfloat16 [2048, 65536], P(None, ('expert', 'feat'))
- reconstruction: float32 [2048, 2304], P(('expert', 'feat'))
The draws below stay inside these ranges and needn't reach their ends.
Inputs may be any that keep to these rules, and one draw needn't show every extreme that they name: `expert_ids`: each row names 8 different experts. Within each aligned block of 16 rows (the rows of one device) no expert is named by more than 2 rows, a bound that some block reaches.
All inputs are finite; a program needn't handle non-finite values.
Results may differ from the reference program's by a relative error of at most 0.012.
Values may be sent and summed in bfloat16 or wider, within the bound.
A program may use at most 128 MiB of HBM per device.

```python
import math
import jax
import jax.numpy as jnp
import numpy as np
from jax import lax

D = 2304
HID = 1024
SHARED = 1024
TOP = 8
TOK_DEV = 16
EXPERTS = 128
FEATURES = 65536
TOKENS = 2048
CAP = 2
N_EXPERT = 16
N_FEAT = 8


def levels(stream_key, dims, cuts, low, largest):
    factor_of, own = 1.0, jax.random.fold_in(stream_key, 6)
    for dim, blocks in cuts:
        steps = jnp.exp(jax.random.uniform(jax.random.fold_in(own, dim), (blocks,), jnp.float32, low / len(cuts), largest / len(cuts)))
        factor_of = factor_of * jnp.repeat(steps, dims[dim] // blocks).reshape([-1 if axis == dim else 1 for axis in range(len(dims))])
    return factor_of


def deal_out(own_key, own, number, rows, number_of, top, most, skew):
    sequence = jax.random.permutation(own_key, number_of)
    heavy_load, common = load_shares(number_of, rows * top, most, skew, True), load_shares(number_of, rows * top, most, skew, False)
    places = jnp.arange(number_of)

    def named(sizes, turn):
        used = int((sizes > 0).sum())
        fixed = max(1, used // 4)
        moved = fixed + (places - fixed + turn * (used - fixed)) % max(1, number_of - fixed)
        return jnp.zeros((number_of,), jnp.int32).at[sequence[jnp.where(places < fixed, places, moved)]].set(jnp.asarray(sizes, jnp.int32))

    sizes = jnp.where(number % 4 == 0, named(heavy_load, number // 4), named(common, number - number // 4 - 1))
    mixed = jax.random.permutation(jax.random.fold_in(own, 3), number_of)
    donor, sink = mixed[0:number_of // 2 * 2:2], mixed[1:number_of // 2 * 2:2]
    room = jnp.minimum(sizes[donor] - 1, most - sizes[sink]) // 2
    room = jnp.where((donor == sequence[0]) | (sink == sequence[0]) | (sizes[sink] == 0), 0, jnp.maximum(room, 0))
    moved = jax.random.randint(jax.random.fold_in(own, 4), (number_of // 2,), 0, 1 << 20) % (room + 1)
    sizes = sizes.at[donor].add(-moved).at[sink].add(moved)
    members = jnp.searchsorted(jnp.cumsum(sizes), jnp.arange(rows * top), side="right").astype(jnp.int32)
    table = members.reshape(top, rows).T
    table = table[jax.random.permutation(jax.random.fold_in(own, 1), rows)]
    turn = jax.random.randint(jax.random.fold_in(own, 2), (rows, 1), 0, top)
    return jnp.take_along_axis(table, (jnp.arange(top)[None, :] + turn) % top, axis=1)


def load_shares(amount, total, most, skew, full):
    portions = [(1 << 20) // math.isqrt(grade ** skew) + 1 for grade in range(1, amount + 1)]
    largest = most if full else min(most, max(-(-total // amount), total * portions[0] // sum(portions)))
    least = 1 if total - largest >= amount - 1 else 0
    given, surplus = [largest] + [least] * (amount - 1), total - largest - least * (amount - 1)
    while surplus > 0:
        free = [i for i in range(1, amount) if given[i] < largest] or [i for i in range(1, amount) if given[i] < most]
        pool, remaining = sum([portions[i] for i in free]), surplus
        for i in free:
            addition = min(most - given[i], max(1, remaining * portions[i] // pool), surplus)
            given[i] = given[i] + addition
            surplus = surplus - addition
    return np.array(given)


def noise(own_key, dims, width, most, split=(), held_as=jnp.bfloat16):
    drawn = width * jax.random.normal(own_key, dims, jnp.float32)
    if split:
        drawn = drawn * levels(own_key, dims, split, -0.22, 0.18)
    return jnp.clip(drawn, -most, most).astype(held_as)


def setup_inputs(seed: int = 0) -> dict:
    splits = jax.random.split(jax.random.key(seed), 14)
    tokens = noise(splits[0], (TOKENS, D), 1.0, 6.0, ((0, 16),))
    expert_ids_keys = jax.random.split(jax.random.fold_in(splits[1], 1), TOKENS // TOK_DEV)
    expert_ids_turns = jax.random.permutation(jax.random.fold_in(splits[1], 3), TOKENS // TOK_DEV)
    expert_ids = jax.vmap(lambda own, number: deal_out(jax.random.fold_in(splits[1], 2), own, number, TOK_DEV, EXPERTS, TOP, CAP, 2))(expert_ids_keys, expert_ids_turns).reshape((TOKENS, TOP))
    gate_weights = jnp.clip(0.1 + 0.5 * jax.random.uniform(splits[2], (TOKENS, TOP), jnp.float32) ** levels(splits[2], (TOKENS, TOP), ((0, 128),), -0.2, 0.2), 0.1, 0.6)
    expert_gate = noise(splits[3], (EXPERTS, D, HID), D ** -0.5, 0.125, ((0, 128),))
    expert_up = noise(splits[4], (EXPERTS, D, HID), D ** -0.5, 0.125, ((0, 128),))
    expert_down = noise(splits[5], (EXPERTS, HID, D), HID ** -0.5, 0.1875, ((0, 128),))
    shared_gate = noise(splits[6], (D, SHARED), D ** -0.5, 0.125, ((1, 8),))
    shared_up = noise(splits[7], (D, SHARED), D ** -0.5, 0.125, ((1, 8),))
    shared_down = noise(splits[8], (SHARED, D), SHARED ** -0.5, 0.1875, ((0, 8),))
    encoder = noise(splits[9], (D, FEATURES), D ** -0.5, 0.125, ((1, 128),))
    encoder_bias = jnp.clip(-0.6 + 0.8 * jax.random.uniform(splits[10], (FEATURES,), jnp.float32) ** levels(splits[10], (FEATURES,), ((0, 128),), -0.2, 0.2), -0.6, 0.2)
    decoder = noise(splits[11], (FEATURES, D), FEATURES ** -0.5, 0.0234375, ((0, 128),))
    decoder_bias = noise(splits[12], (D,), 0.5, 3.0, (), jnp.float32)
    return dict(tokens=tokens, expert_ids=expert_ids, gate_weights=gate_weights, expert_gate=expert_gate, expert_up=expert_up, expert_down=expert_down, shared_gate=shared_gate, shared_up=shared_up, shared_down=shared_down, encoder=encoder, encoder_bias=encoder_bias, decoder=decoder, decoder_bias=decoder_bias)


def swiglu_block(row_block, weight_gate, weight_up, weight_down):
    gate_proj = jnp.dot(row_block, weight_gate, preferred_element_type=jnp.float32)
    up_proj = jnp.dot(row_block, weight_up, preferred_element_type=jnp.float32)
    hidden = (jax.nn.silu(gate_proj) * up_proj).astype(jnp.bfloat16)
    return jnp.dot(hidden, weight_down, preferred_element_type=jnp.float32).astype(jnp.bfloat16)


def reference(tokens, expert_ids, gate_weights, expert_gate, expert_up, expert_down, shared_gate, shared_up, shared_down, encoder, encoder_bias, decoder, decoder_bias):
    devices = N_EXPERT * N_FEAT
    pair_count = TOK_DEV * TOP
    blocks = expert_ids.reshape(devices, pair_count).astype(jnp.int32)
    onehot = (blocks[:, :, None] == jnp.arange(EXPERTS, dtype=jnp.int32)[None, None, :]).astype(jnp.int32)
    earlier = (jnp.cumsum(onehot, axis=1) - onehot).astype(jnp.int32)
    slot_index = jnp.sum(earlier * onehot, axis=2).astype(jnp.int32)
    source = jnp.arange(devices, dtype=jnp.int32)[:, None]
    row_place = ((blocks * devices + source) * CAP + slot_index).reshape(-1).astype(jnp.int32)
    token_index = jnp.repeat(jnp.arange(TOKENS, dtype=jnp.int32), TOP)
    token_table = jnp.full((EXPERTS * devices * CAP,), TOKENS, jnp.int32).at[row_place].set(token_index)
    padded = jnp.concatenate([tokens, jnp.zeros((1, D), tokens.dtype)], axis=0)

    def one_expert(operands):
        index_rows, weight_gate, weight_up, weight_down = operands
        return swiglu_block(padded[index_rows], weight_gate, weight_up, weight_down)

    outputs = lax.map(one_expert, (token_table.reshape(EXPERTS, devices * CAP), expert_gate, expert_up, expert_down))
    gathered = outputs.reshape(-1, D)[row_place].reshape(TOKENS, TOP, D)
    routed = jnp.einsum("tk,tkd->td", gate_weights.astype(jnp.float32), gathered.astype(jnp.float32), precision=lax.Precision.HIGHEST).astype(jnp.bfloat16)
    shared = swiglu_block(tokens, shared_gate, shared_up, shared_down)
    moe_out = (routed.astype(jnp.float32) + shared.astype(jnp.float32)).astype(jnp.bfloat16)
    features = jax.nn.relu(jnp.dot(moe_out, encoder, preferred_element_type=jnp.float32) + encoder_bias[None, :]).astype(jnp.bfloat16)
    reconstruction = jnp.dot(features, decoder, preferred_element_type=jnp.float32) + decoder_bias[None, :]
    return features, reconstruction
```

```python
import functools

import jax
import jax.numpy as jnp
from jax import lax
from jax.experimental import pallas as pl
from jax.experimental.pallas import tpu as pltpu
from jax.sharding import PartitionSpec as P

MESH = pl.DeviceIdType.MESH
SIDE = 4
ORDERS = ((1, 0, 2), (0, 2, 1), (2, 1, 0))
PARTS = len(ORDERS)
ALL = slice(None)


def sae_kernel(
    rows_ref, enc_hbm, bias_ref, dec_hbm, dec_bias_ref, feat_hbm, rec_ref,
    gathered, feats, enc, dec, out_half, in_half, total, land0, land1, land2,
    ag_send, ag_recv, cross_send, cross_recv, half_send, half_recv, rs_send, rs_recv, local_sem, feat_sem,
):
    e, f = lax.axis_index("expert"), lax.axis_index("feat")
    core = lax.rem(f, 2)
    other = 1 - core
    pos = (e // SIDE, lax.rem(e, SIDE), f // 2)
    lands = (land0, land1, land2)
    width = gathered.shape[-1]
    hid = width // 2

    def at(axis, delta):
        return lax.rem(pos[axis] + delta + SIDE, SIDE)

    def device(axis, delta):
        there = list(pos)
        there[axis] = at(axis, delta)
        return (there[0] * SIDE + there[1], there[2] * 2 + core)

    partner = (e, f + 1 - 2 * core)

    def remote(src, dst, send, recv, where):
        return pltpu.make_async_remote_copy(
            src_ref=src, dst_ref=dst, send_sem=send, recv_sem=recv, device_id=where, device_id_type=MESH
        )

    locals_ = [
        pltpu.make_async_copy(enc_hbm, enc, local_sem.at[0]),
        pltpu.make_async_copy(dec_hbm, dec, local_sem.at[1]),
    ]
    for part in range(PARTS):
        locals_.append(
            pltpu.make_async_copy(
                rows_ref.at[:, pl.ds(part * width, width)],
                gathered.at[part, core, pos[0], pos[1], pos[2]],
                local_sem.at[2 + part],
            )
        )
    for copy in locals_:
        copy.start()

    barrier = pltpu.get_barrier_semaphore()
    neighbours = [device(axis, delta) for axis in range(3) for delta in (1, -1)] + [partner]
    for there in neighbours:
        pl.semaphore_signal(barrier, inc=1, device_id=there, device_id_type=MESH)
    pl.semaphore_wait(barrier, len(neighbours))

    def ag_cells(part, stage, k, half, which):
        order = ORDERS[part]
        idx = list(pos)
        for axis in order[:stage]:
            idx[axis] = ALL
        idx[order[stage]] = k
        cols = ALL
        if half is not None:
            if stage:
                idx[order[0]] = pl.ds(2 * half, 2)
            else:
                cols = pl.ds(hid * half, hid)
        return gathered.at[(part, which, *idx, ALL, cols)]

    ag = {}

    def ag_start(part, stage, j, src, k, half, delta):
        copy = remote(
            src,
            ag_cells(part, stage, k, half, core),
            ag_send.at[stage, part, j],
            ag_recv.at[stage, part, j],
            device(ORDERS[part][stage], delta),
        )
        copy.start()
        ag[part, stage, j] = copy

    AG_FROM = ((-1, 0), (1, 1), (-1, 1), (1, 0), (-2, 0), (2, 1))

    def ag_landed(part, stage, j):
        delta, half = AG_FROM[j]
        cells = ag_cells(part, stage, at(ORDERS[part][stage], delta), half, core)
        remote(
            cells, cells, ag_send.at[stage, part, j], ag_recv.at[stage, part, j],
            device(ORDERS[part][stage], 1),
        ).wait_recv()
        return cells

    cross = []

    def cross_start(part, j, cells):
        copy = remote(cells, cells, cross_send.at[part, j], cross_recv.at[part, j], partner)
        copy.start()
        cross.append(copy)

    for stage in range(3):
        for part in range(PARTS):
            axis = ORDERS[part][stage]
            here = pos[axis]
            for j, (delta, half) in enumerate(((1, 0), (-1, 1), (1, 1), (-1, 0))):
                if stage == 0:
                    src = rows_ref.at[:, pl.ds(part * width + hid * half, hid)]
                else:
                    src = ag_cells(part, stage, here, half, core)
                ag_start(part, stage, j, src, here, half, delta)
            if stage == 2:
                cross_start(part, 6, ag_cells(part, stage, here, None, core))
        for part in range(PARTS):
            axis = ORDERS[part][stage]
            for j, delta in ((0, 1), (1, -1)):
                cells = ag_landed(part, stage, j)
                ag_start(part, stage, 4 + j, cells, at(axis, -delta), AG_FROM[j][1], delta)
                if stage == 2:
                    cross_start(part, j, cells)
        for j in (2, 3, 4, 5):
            for part in range(PARTS):
                cells = ag_landed(part, stage, j)
                if stage == 2:
                    cross_start(part, j, cells)
        if stage == 0:
            for copy in locals_:
                copy.wait()
    for part in range(PARTS):
        axis = ORDERS[part][2]
        for j in range(7):
            delta, half = AG_FROM[j] if j < 6 else (0, None)
            cells = ag_cells(part, 2, at(axis, delta), half, other)
            remote(cells, cells, cross_send.at[part, j], cross_recv.at[part, j], partner).wait_recv()

    features = enc.shape[1]

    def encode(step, carry):
        which, y = step // 2, 2 * lax.rem(step, 2)
        rows = 2 * SIDE * SIDE * 16
        scores = bias_ref[...].astype(jnp.float32)
        for part in range(PARTS):
            block = gathered[part, which, pl.ds(y, 2)].reshape(rows, width)
            scores = scores + jnp.dot(
                block, enc[part * width : (part + 1) * width, :], preferred_element_type=jnp.float32
            )
        feats[which, pl.ds(y, 2)] = (
            jnp.maximum(scores, 0.0).astype(jnp.bfloat16).reshape(2, SIDE, SIDE, 16, features)
        )
        return carry

    lax.fori_loop(0, 4, encode, 0)
    feat_copies = []
    for which in range(2):
        copy = pltpu.make_async_copy(feats.at[which], feat_hbm.at[:, :, :, which], feat_sem.at[which])
        copy.start()
        feat_copies.append(copy)

    def cells_of(part, stage, k, half):
        order = ORDERS[part]
        left = order[: 2 - stage]
        idx = list(pos)
        for axis in left:
            idx[axis] = ALL
        idx[order[2 - stage]] = k
        cols = ALL
        if half is not None:
            if left:
                idx[order[0]] = pl.ds(2 * half, 2)
            else:
                cols = pl.ds(hid * half, hid)
        return (*idx, ALL, cols)

    def land_of(part, stage, kind, half):
        order = ORDERS[part]
        left = sorted(order[: 2 - stage])
        idx = [ALL for _ in left]
        cols = ALL
        if half is not None:
            if left:
                idx[left.index(order[0])] = pl.ds(2 * half, 2)
            else:
                cols = pl.ds(hid * half, hid)
        return (part, kind, *idx, ALL, cols)

    def product(part, delta, which):
        idx = cells_of(part, 0, at(ORDERS[part][2], delta), None)
        block = feats[(which, *idx)].reshape(SIDE * SIDE * 16, features)
        return jnp.dot(
            block, dec[:, part * width : (part + 1) * width], preferred_element_type=jnp.float32
        ).reshape(SIDE, SIDE, 16, width)

    halves = []

    def half_copy(part, delta):
        idx = cells_of(part, 0, at(ORDERS[part][2], delta), None)
        return remote(
            out_half.at[(part, *idx)],
            in_half.at[(part, *idx)],
            half_send.at[part, delta + 1],
            half_recv.at[part, delta + 1],
            partner,
        )

    def give(part, delta):
        idx = cells_of(part, 0, at(ORDERS[part][2], delta), None)
        out_half[(part, *idx)] = product(part, delta, other).astype(jnp.bfloat16)
        copy = half_copy(part, delta)
        copy.start()
        halves.append(copy)

    def keep(part, delta):
        idx = cells_of(part, 0, at(ORDERS[part][2], delta), None)
        mine = product(part, delta, core)
        half_copy(part, delta).wait_recv()
        total[(part, *idx)] = (mine + in_half[(part, *idx)].astype(jnp.float32)).astype(jnp.bfloat16)

    MINUS, PLUS, FAR = 0, 1, 2
    RS_COPIES = (
        (2, 0, 1, FAR), (2, 1, -1, FAR), (1, 1, 1, MINUS), (-1, 0, -1, PLUS), (1, 0, 1, MINUS), (-1, 1, -1, PLUS),
    )
    rs = []

    def rs_copy(part, stage, j):
        delta, half, way, kind = RS_COPIES[j]
        axis = ORDERS[part][2 - stage]
        return remote(
            total.at[(part, *cells_of(part, stage, at(axis, delta), half))],
            lands[stage].at[land_of(part, stage, kind, half)],
            rs_send.at[stage, part, j],
            rs_recv.at[stage, part, j],
            device(axis, way),
        )

    def rs_start(part, stage, j):
        copy = rs_copy(part, stage, j)
        copy.start()
        rs.append(copy)

    def pass_on(part, stage):
        for j in (0, 1):
            rs_copy(part, stage, j).wait_recv()
            _, half, way, _ = RS_COPIES[j]
            idx = (part, *cells_of(part, stage, at(ORDERS[part][2 - stage], way), half))
            far = lands[stage][land_of(part, stage, FAR, half)]
            total[idx] = (total[idx].astype(jnp.float32) + far.astype(jnp.float32)).astype(jnp.bfloat16)
            rs_start(part, stage, 4 + j)

    def own_sum(part, stage):
        for j in (2, 3, 4, 5):
            rs_copy(part, stage, j).wait_recv()
        idx = (part, *cells_of(part, stage, pos[ORDERS[part][2 - stage]], None))
        value = total[idx].astype(jnp.float32)
        for kind in (MINUS, PLUS):
            value = value + lands[stage][land_of(part, stage, kind, None)].astype(jnp.float32)
        return idx, value

    for part in range(PARTS):
        give(part, 2)
    for part in range(PARTS):
        keep(part, 2)
        rs_start(part, 0, 0)
        rs_start(part, 0, 1)
    for part in range(PARTS):
        give(part, 1)
        give(part, -1)
    for part in range(PARTS):
        keep(part, 1)
        rs_start(part, 0, 2)
        keep(part, -1)
        rs_start(part, 0, 3)
    for part in range(PARTS):
        give(part, 0)
    for part in range(PARTS):
        pass_on(part, 0)
    for part in range(PARTS):
        keep(part, 0)
    for stage in range(3):
        if stage:
            for part in range(PARTS):
                pass_on(part, stage)
        for part in range(PARTS):
            idx, value = own_sum(part, stage)
            if stage < 2:
                total[idx] = value.astype(jnp.bfloat16)
                for j in range(4):
                    rs_start(part, stage + 1, j)
            else:
                cols = slice(part * width, (part + 1) * width)
                rec_ref[:, cols] = value + dec_bias_ref[:, cols]

    for copy in list(ag.values()) + cross + halves + rs:
        copy.wait_send()
    for copy in feat_copies:
        copy.wait()


def sae(rows, encoder, encoder_bias, decoder, decoder_bias):
    own_rows, model = rows.shape
    features = encoder.shape[1]
    width = model // PARTS
    cube = (SIDE, SIDE, SIDE)
    bf16 = jnp.bfloat16
    vmem = pl.BlockSpec(memory_space=pltpu.VMEM)
    hbm = pl.BlockSpec(memory_space=pl.ANY)
    dma = pltpu.SemaphoreType.DMA
    out, rec = pl.pallas_call(
        sae_kernel,
        name="sae",
        out_shape=(
            jax.ShapeDtypeStruct((*cube, 2, own_rows, features), bf16),
            jax.ShapeDtypeStruct((own_rows, model), jnp.float32),
        ),
        in_specs=[vmem, hbm, vmem, hbm, vmem],
        out_specs=(hbm, vmem),
        scratch_shapes=[
            pltpu.VMEM((PARTS, 2, *cube, own_rows, width), bf16),
            pltpu.VMEM((2, *cube, own_rows, features), bf16),
            pltpu.VMEM((model, features), bf16),
            pltpu.VMEM((features, model), bf16),
            pltpu.VMEM((PARTS, *cube, own_rows, width), bf16),
            pltpu.VMEM((PARTS, *cube, own_rows, width), bf16),
            pltpu.VMEM((PARTS, *cube, own_rows, width), bf16),
            pltpu.VMEM((PARTS, 3, SIDE, SIDE, own_rows, width), bf16),
            pltpu.VMEM((PARTS, 3, SIDE, own_rows, width), bf16),
            pltpu.VMEM((PARTS, 3, own_rows, width), bf16),
            dma((3, PARTS, 6)),
            dma((3, PARTS, 6)),
            dma((PARTS, 7)),
            dma((PARTS, 7)),
            dma((PARTS, 4)),
            dma((PARTS, 4)),
            dma((3, PARTS, 6)),
            dma((3, PARTS, 6)),
            dma((2 + PARTS,)),
            dma((2,)),
        ],
        compiler_params=pltpu.CompilerParams(
            collective_id=0, has_side_effects=True, vmem_limit_bytes=60 * 1024 * 1024
        ),
    )(rows, encoder, encoder_bias[None, :], decoder, decoder_bias[None, :])
    return out.reshape(-1, features), rec


def run_experts(received, expert_gate, expert_up, expert_down):
    gate_proj = jnp.einsum(
        "sjcd,jdh->sjch", received, expert_gate, preferred_element_type=jnp.float32
    )
    up_proj = jnp.einsum("sjcd,jdh->sjch", received, expert_up, preferred_element_type=jnp.float32)
    hidden = (jax.nn.silu(gate_proj) * up_proj).astype(jnp.bfloat16)
    return jnp.einsum(
        "sjch,jhd->sjcd", hidden, expert_down, preferred_element_type=jnp.float32
    ).astype(jnp.bfloat16)


def shards(
    tokens,
    expert_ids,
    gate_weights,
    expert_gate,
    expert_up,
    expert_down,
    shared_gate,
    shared_up,
    shared_down,
    encoder,
    encoder_bias,
    decoder,
    decoder_bias,
):
    devices = lax.axis_size(("expert", "feat"))
    own_rows = expert_ids.shape[0]
    top_count = expert_ids.shape[1]
    width = tokens.shape[1]
    local_experts = expert_gate.shape[0]
    experts = local_experts * devices
    cap_slots = max(2, 2 * own_rows * top_count // experts)
    my_tokens = lax.dynamic_slice_in_dim(tokens, lax.axis_index("feat") * own_rows, own_rows, 0)
    flat_ids = expert_ids.reshape(-1)
    onehot = (flat_ids[:, None] == jnp.arange(experts, dtype=jnp.int32)[None, :]).astype(jnp.int32)
    earlier = jnp.cumsum(onehot, axis=0) - onehot
    slot_index = jnp.sum(earlier * onehot, axis=1)
    places = flat_ids * cap_slots + slot_index
    token_owner = jnp.repeat(jnp.arange(own_rows, dtype=jnp.int32), top_count)
    place_hot = (
        places[:, None] == jnp.arange(experts * cap_slots, dtype=jnp.int32)[None, :]
    ).astype(jnp.float32)
    token_hot = (token_owner[:, None] == jnp.arange(own_rows, dtype=jnp.int32)[None, :]).astype(
        jnp.float32
    )
    dispatch_map = jnp.einsum("ps,pt->st", place_hot, token_hot).astype(jnp.bfloat16)
    weighted_hot = token_hot * gate_weights.reshape(-1)[:, None]
    combine_map = jnp.einsum("pt,ps->ts", weighted_hot, place_hot, precision=lax.Precision.HIGHEST)
    outgoing = jnp.dot(dispatch_map, my_tokens, preferred_element_type=jnp.float32).astype(
        jnp.bfloat16
    )
    outgoing = outgoing.reshape(devices, local_experts, cap_slots, width)
    served = run_experts(
        lax.all_to_all(outgoing, ("expert", "feat"), split_axis=0, concat_axis=0, tiled=True),
        expert_gate,
        expert_up,
        expert_down,
    )
    returned = lax.all_to_all(served, ("expert", "feat"), split_axis=0, concat_axis=0, tiled=True)
    returned_rows = returned.reshape(experts * cap_slots, width).astype(jnp.float32)
    routed = jnp.dot(combine_map, returned_rows, precision=lax.Precision.HIGHEST).astype(
        jnp.bfloat16
    )
    shared_gate_proj = jnp.dot(tokens, shared_gate, preferred_element_type=jnp.float32)
    shared_up_proj = jnp.dot(tokens, shared_up, preferred_element_type=jnp.float32)
    shared_hidden = (jax.nn.silu(shared_gate_proj) * shared_up_proj).astype(jnp.bfloat16)
    block_rows = shared_hidden
    shared_out = lax.psum_scatter(
        jnp.dot(block_rows, shared_down, preferred_element_type=jnp.float32),
        "feat",
        scatter_dimension=0,
        tiled=True,
    ).astype(jnp.bfloat16)
    moe_out = (routed.astype(jnp.float32) + shared_out.astype(jnp.float32)).astype(jnp.bfloat16)
    return sae(moe_out, encoder, encoder_bias, decoder, decoder_bias)


def solution(mesh):
    return jax.shard_map(
        shards,
        mesh=mesh,
        in_specs=(
            P("expert", None),
            P(("expert", "feat"), None),
            P(("expert", "feat"), None),
            P(("expert", "feat"), None, None),
            P(("expert", "feat"), None, None),
            P(("expert", "feat"), None, None),
            P(None, "feat"),
            P(None, "feat"),
            P("feat", None),
            P(None, ("expert", "feat")),
            P(("expert", "feat")),
            P(("expert", "feat"), None),
            P(),
        ),
        out_specs=(P(None, ("expert", "feat")), P(("expert", "feat"), None)),
        check_vma=False,
    )
```

```python
import jax
import jax.numpy as jnp
from jax import lax
from jax.experimental import pallas as pl
from jax.experimental.pallas import tpu as pltpu
from jax.sharding import PartitionSpec as P

MESH = pl.DeviceIdType.MESH
SIDE = 4
ORDERS = ((1, 0, 2), (0, 2, 1), (2, 1, 0))
PARTS = len(ORDERS)
ALL = slice(None)
BF16 = jnp.bfloat16
F32 = jnp.float32
OUTWARD = (0, 1, -1, 2)
INWARD = (2, 1, -1, 0)
FAR_WAY = {0: 1, 2: 1, 1: -1, -1: -1}
FAR, MINUS, PLUS = 0, 1, 2
OTHERS = (1, -1, 2)
TOP = 8
COPIES = 18


class Torus:
    def __init__(self):
        self.e, self.f = lax.axis_index("expert"), lax.axis_index("feat")
        self.core = lax.rem(self.f, 2)
        self.other = 1 - self.core
        self.pos = (self.e // SIDE, lax.rem(self.e, SIDE), self.f // 2)
        self.partner = (self.e, self.f + 1 - 2 * self.core)

    def at(self, axis, delta):
        return lax.rem(self.pos[axis] + delta + SIDE, SIDE) if delta else self.pos[axis]

    def device(self, axis, delta):
        there = list(self.pos)
        there[axis] = self.at(axis, delta)
        return (there[0] * SIDE + there[1], there[2] * 2 + self.core)

    def index(self, part, offsets):
        idx = [None] * 3
        for axis, delta in zip(ORDERS[part], offsets):
            idx[axis] = ALL if delta is None else self.at(axis, delta)
        return tuple(idx)

    def meet(self, peers):
        barrier = pltpu.get_barrier_semaphore()
        for there in peers:
            pl.semaphore_signal(barrier, inc=1, device_id=there, device_id_type=MESH)
        pl.semaphore_wait(barrier, len(peers))


def remote(src, dst, send, recv, where):
    return pltpu.make_async_remote_copy(
        src_ref=src, dst_ref=dst, send_sem=send, recv_sem=recv, device_id=where, device_id_type=MESH
    )


class Gather:
    def __init__(self, torus, own, buf, send, recv):
        self.torus, self.own, self.buf, self.send, self.recv = torus, own, buf, send, recv
        self.specs = [(0, d, (0, 0, 0), (-d, 0, 0)) for d in OTHERS]
        self.specs += [(1, d, (None, 0, 0), (None, -d, 0)) for d in OTHERS]
        for d in OUTWARD:
            way = FAR_WAY[d]
            self.specs += [
                (2, 1, (None, d, 0), (None, d, -1)),
                (2, -1, (None, d, 0), (None, d, 1)),
                (2, way, (None, d, -way), (None, d, 2)),
            ]
        self.started = []

    def cells(self, part, offsets):
        return self.buf.at[(part, *self.torus.index(part, offsets))]

    def copy(self, part, k, landing):
        slot, delta, source, target = self.specs[k]
        dst = self.cells(part, target if landing else source)
        src = self.own(part) if source == (0, 0, 0) and not landing else dst
        return remote(
            src, dst, self.send.at[part, k], self.recv.at[part, k], self.torus.device(ORDERS[part][slot], delta)
        )

    def start(self, part, *ks):
        for k in ks:
            copy = self.copy(part, k, False)
            copy.start()
            self.started.append(copy)

    def wait(self, part, *ks):
        for k in ks:
            self.copy(part, k, True).wait_recv()

    def run(self, own_ready):
        parts = range(PARTS)
        plane = {d: 6 + 3 * i for i, d in enumerate(OUTWARD)}
        for p in parts:
            self.start(p, 0, 1, 2)
        own_ready()
        for p in parts:
            self.wait(p, 0, 1, 2)
            self.start(p, 3, 4, 5)
        for p in parts:
            self.start(p, plane[0], plane[0] + 1)
        for i, d in enumerate(OTHERS):
            for p in parts:
                self.wait(p, 3 + i)
                self.start(p, plane[-d if d != 2 else 2], plane[-d if d != 2 else 2] + 1)
            if i == 1:
                for p in parts:
                    self.wait(p, plane[0], plane[0] + 1)
                    self.start(p, plane[0] + 2)
        for d in (-1, 1, 2):
            for p in parts:
                self.wait(p, plane[d], plane[d] + 1)
                self.start(p, plane[d] + 2)
        for p in parts:
            for d in OUTWARD:
                self.wait(p, plane[d] + 2)

    def drain(self):
        for copy in self.started:
            copy.wait_send()


class Scatter:
    def __init__(self, torus, total, planes, lines, blocks, send, recv):
        self.torus, self.total, self.send, self.recv = torus, total, send, recv
        self.specs = []
        for i, d in enumerate(INWARD):
            for way, last, kind in ((FAR_WAY[d], 2, FAR), (1, 1, MINUS), (-1, -1, PLUS)):
                self.specs.append((2, way, (None, d, last), planes, (kind, i)))
        self.specs += [(1, d, (None, d, 0), lines, (i,)) for i, d in enumerate(INWARD[:3])]
        self.specs += [(0, d, (d, 0, 0), blocks, (i,)) for i, d in enumerate(INWARD[:3])]
        self.started = []

    def cells(self, part, offsets):
        return (part, *self.torus.index(part, offsets))

    def copy(self, part, k):
        slot, delta, source, lands, place = self.specs[k]
        return remote(
            self.total.at[self.cells(part, source)],
            lands.at[(part, *place)],
            self.send.at[part, k],
            self.recv.at[part, k],
            self.torus.device(ORDERS[part][slot], delta),
        )

    def start(self, part, *ks):
        for k in ks:
            copy = self.copy(part, k)
            copy.start()
            self.started.append(copy)

    def landed(self, part, k):
        self.copy(part, k).wait_recv()
        _, _, _, lands, place = self.specs[k]
        return lands[(part, *place)].astype(F32)

    def add(self, part, offsets, ks):
        idx = self.cells(part, offsets)
        value = self.total[idx].astype(F32)
        for k in ks:
            value = value + self.landed(part, k)
        return idx, value

    def run(self, produce, finish):
        parts = range(PARTS)
        plane = {d: 3 * i for i, d in enumerate(INWARD)}

        def raw(p, way):
            for d in INWARD:
                if FAR_WAY[d] != way:
                    self.start(p, plane[d] + (1 if way == 1 else 2))

        for p in parts:
            produce(p, 2)
            self.start(p, *(plane[d] for d in INWARD))
        for p in parts:
            produce(p, 1)
            raw(p, 1)
            produce(p, -1)
            raw(p, -1)
        for p in parts:
            produce(p, 0)
        for d in INWARD:
            way = FAR_WAY[d]
            for p in parts:
                idx, value = self.add(p, (None, d, way), (plane[d],))
                self.total[idx] = value.astype(BF16)
                self.start(p, plane[d] + (1 if way == 1 else 2))
        for i, d in enumerate(INWARD):
            for p in parts:
                idx, value = self.add(p, (None, d, 0), (plane[d] + 1, plane[d] + 2))
                self.total[idx] = value.astype(BF16)
                if d:
                    self.start(p, 12 + i)
        for p in parts:
            idx, value = self.add(p, (None, 0, 0), (12, 13, 14))
            self.total[idx] = value.astype(BF16)
            self.start(p, 15, 16, 17)
        for p in parts:
            _, value = self.add(p, (0, 0, 0), (15, 16, 17))
            finish(p, value)

    def drain(self):
        for copy in self.started:
            copy.wait_send()


def torus_scratch(rows, width):
    cube = (SIDE, SIDE, SIDE)
    dma = pltpu.SemaphoreType.DMA((PARTS, COPIES))
    return [
        pltpu.VMEM((PARTS, *cube, rows, width), BF16),
        pltpu.VMEM((PARTS, *cube, rows, width), BF16),
        pltpu.VMEM((PARTS, 3, SIDE, SIDE, rows, width), BF16),
        pltpu.VMEM((PARTS, 3, SIDE, rows, width), BF16),
        pltpu.VMEM((PARTS, 3, rows, width), BF16),
        dma, dma, dma, dma,
    ]


def sae_kernel(
    rows_ref, enc_hbm, bias_ref, dec_hbm, dec_bias_ref, feat_hbm, rec_ref,
    gathered, total, planes, lines, blocks, ag_send, ag_recv, rs_send, rs_recv,
    feats, enc, dec, bias, local_sem, cross_send, cross_recv,
):
    torus = Torus()
    core, other, partner = torus.core, torus.other, torus.partner
    width = gathered.shape[-1]
    features = enc.shape[2]

    own_copies = [
        pltpu.make_async_copy(
            rows_ref.at[:, pl.ds(p * width, width)], gathered.at[(p, *torus.pos)], local_sem.at[p]
        )
        for p in range(PARTS)
    ]
    weight_copies = [
        pltpu.make_async_copy(src, dst.at[core], local_sem.at[PARTS + i])
        for i, (src, dst) in enumerate(((enc_hbm, enc), (bias_ref, bias), (dec_hbm, dec)))
    ]
    for copy in own_copies + weight_copies:
        copy.start()
    torus.meet([torus.device(axis, d) for axis in range(3) for d in OTHERS] + [partner])

    shared_copies = [
        remote(src, dst.at[core], cross_send.at[i], cross_recv.at[i], partner)
        for i, (src, dst) in enumerate(((enc_hbm, enc), (bias_ref, bias), (dec_hbm, dec)))
    ]

    def own_ready():
        for copy in own_copies:
            copy.wait()
        for copy in shared_copies:
            copy.start()

    gather = Gather(torus, lambda p: rows_ref.at[:, pl.ds(p * width, width)], gathered, ag_send, ag_recv)
    gather.run(own_ready)
    for copy in weight_copies:
        copy.wait()
    for copy in shared_copies:
        copy.wait_recv()
    def encode(step, carry):
        which, y = step // 2, 2 * lax.rem(step, 2)
        rows = 2 * SIDE * SIDE * 16
        scores = bias[which]
        for p in range(PARTS):
            block = gathered[p, pl.ds(y, 2)].reshape(rows, width)
            scores = scores + jnp.dot(
                block, enc[which, p * width : (p + 1) * width, :], preferred_element_type=F32
            )
        feats[which, pl.ds(y, 2)] = (
            jnp.maximum(scores, 0.0).astype(BF16).reshape(2, SIDE, SIDE, 16, features)
        )
        return carry

    lax.fori_loop(0, 4, encode, 0)
    own_out = pltpu.make_async_copy(feats.at[core], feat_hbm.at[:, :, :, core], local_sem.at[PARTS + 3])
    cross_out = remote(
        feats.at[other], feat_hbm.at[:, :, :, core], cross_send.at[3], cross_recv.at[3], partner
    )
    cross_in = remote(
        feats.at[other], feat_hbm.at[:, :, :, other], cross_send.at[3], cross_recv.at[3], partner
    )
    own_out.start()
    cross_out.start()

    scatter = Scatter(torus, total, planes, lines, blocks, rs_send, rs_recv)

    def produce(p, delta):
        idx = torus.index(p, (None, None, delta))
        left = [feats[(which, *idx)].reshape(SIDE * SIDE * 16, features) for which in range(2)]
        tile = 256

        def columns(step, carry):
            cols = pl.ds(pl.multiple_of(step * tile, tile), tile)
            here = pl.ds(pl.multiple_of(p * width + step * tile, tile), tile)
            value = jnp.dot(left[0], dec[0, :, here], preferred_element_type=F32) + jnp.dot(
                left[1], dec[1, :, here], preferred_element_type=F32
            )
            total[(p, *idx, ALL, cols)] = value.astype(BF16).reshape(SIDE, SIDE, 16, tile)
            return carry

        lax.fori_loop(0, width // tile, columns, 0)

    def finish(p, value):
        cols = slice(p * width, (p + 1) * width)
        rec_ref[:, cols] = value + dec_bias_ref[:, cols]

    scatter.run(produce, finish)

    own_out.wait()
    cross_out.wait_send()
    cross_in.wait_recv()
    for copy in shared_copies:
        copy.wait_send()
    gather.drain()
    scatter.drain()


def sae(rows, encoder, encoder_bias, decoder, decoder_bias):
    own_rows, model = rows.shape
    features = encoder.shape[1]
    width = model // PARTS
    cube = (SIDE, SIDE, SIDE)
    vmem = pl.BlockSpec(memory_space=pltpu.VMEM)
    hbm = pl.BlockSpec(memory_space=pl.ANY)
    dma = pltpu.SemaphoreType.DMA
    out, rec = pl.pallas_call(
        sae_kernel,
        name="sae",
        out_shape=(
            jax.ShapeDtypeStruct((*cube, 2, own_rows, features), BF16),
            jax.ShapeDtypeStruct((own_rows, model), F32),
        ),
        in_specs=[vmem, hbm, vmem, hbm, vmem],
        out_specs=(hbm, vmem),
        scratch_shapes=torus_scratch(own_rows, width)
        + [
            pltpu.VMEM((2, *cube, own_rows, features), BF16),
            pltpu.VMEM((2, model, features), BF16),
            pltpu.VMEM((2, features, model), BF16),
            pltpu.VMEM((2, 1, features), F32),
            dma((PARTS + 4,)),
            dma((4,)),
            dma((4,)),
        ],
        compiler_params=pltpu.CompilerParams(
            collective_id=0, has_side_effects=True, vmem_limit_bytes=60 * 1024 * 1024
        ),
    )(rows, encoder, encoder_bias[None, :], decoder, decoder_bias[None, :])
    return out.reshape(-1, features), rec


def moe_kernel(
    tokens_ref, meta_ref, gate_hbm, up_hbm, down_hbm, sgate_hbm, sup_hbm, sdown_hbm, out_ref,
    gate, up, down, sgate, sup, sdown, metas, partial, combine, outgoing, received, hidden, served, returned,
    parts_out, parts_in, local_sem, meta_send, meta_recv, go_send, go_recv, back_send, back_recv, part_send, part_recv,
):
    torus = Torus()
    e, f = torus.e, torus.f
    n_e, own_rows, model = outgoing.shape
    n_f = metas.shape[0]
    rows = n_f * own_rows
    slots = n_e * own_rows
    hid = hidden.shape[1]
    tile = 256

    weight_copies = [
        pltpu.make_async_copy(src, dst, local_sem.at[i])
        for i, (src, dst) in enumerate(
            (
                (sgate_hbm, sgate), (sup_hbm, sup), (sdown_hbm, sdown),
                (gate_hbm.at[0], gate), (up_hbm.at[0], up), (down_hbm.at[0], down),
            )
        )
    ]
    own_meta = pltpu.make_async_copy(meta_ref, metas.at[f], local_sem.at[6])
    for copy in weight_copies + [own_meta]:
        copy.start()

    moves = [(dy, dx) for dy in range(SIDE) for dx in range(SIDE) if dy or dx]

    def plane(dy, dx):
        return lax.rem(torus.pos[0] + dy, SIDE) * SIDE + lax.rem(torus.pos[1] + dx, SIDE)

    def column(i):
        return lax.rem(f + i, n_f)

    torus.meet([(plane(*m), f) for m in moves] + [(e, column(i)) for i in range(1, n_f)])

    sent = []

    def send(copy):
        copy.start()
        sent.append(copy)

    for i in range(1, n_f):
        send(remote(meta_ref, metas.at[f], meta_send.at[i - 1], meta_recv.at[i - 1], (e, column(i))))

    for copy in weight_copies[:3]:
        copy.wait()
    tokens = tokens_ref[...]
    shared_gate = jnp.dot(tokens, sgate[...], preferred_element_type=F32)
    shared_up = jnp.dot(tokens, sup[...], preferred_element_type=F32)
    shared_hidden = (jax.nn.silu(shared_gate) * shared_up).astype(BF16)

    own_meta.wait()
    for i in range(1, n_f):
        src = column(n_f - i)
        remote(metas.at[src], metas.at[src], meta_send.at[i - 1], meta_recv.at[i - 1], (e, src)).wait_recv()
    table = metas[...].reshape(rows, metas.shape[2])
    slot = lax.broadcasted_iota(jnp.int32, (rows, slots), 1)
    token = lax.broadcasted_iota(jnp.int32, (rows, slots), 0)
    wanted = ((slot // own_rows) * n_f + f).astype(F32)
    named = jnp.zeros((rows, slots), F32)
    weight = jnp.zeros((rows, slots), F32)
    for k in range(TOP):
        same = table[:, k : k + 1] == wanted
        named = named + jnp.where(same, 1.0, 0.0)
        weight = weight + jnp.where(same, table[:, TOP + k : TOP + k + 1], 0.0)
    row = lax.broadcasted_iota(jnp.int32, (rows, rows), 0)
    col = lax.broadcasted_iota(jnp.int32, (rows, rows), 1)
    before = jnp.where((row // own_rows == col // own_rows) & (col < row), 1.0, 0.0).astype(BF16)
    rank = jnp.dot(before, named.astype(BF16), preferred_element_type=F32)
    here = (lax.rem(slot, 2).astype(F32) == rank) & (lax.rem(slot // 2, n_f) == token // own_rows)
    places = jnp.where(here, named, 0.0)
    weight = places * weight
    high = weight.astype(BF16)
    combine[0] = high
    combine[1] = (weight - high.astype(F32)).astype(BF16)
    dispatch = places.T.astype(BF16)

    def pick(step, carry):
        cols = pl.ds(pl.multiple_of(step * tile, tile), tile)
        value = jnp.dot(dispatch, tokens_ref[:, cols], preferred_element_type=F32)
        outgoing[:, :, cols] = value.astype(BF16).reshape(n_e, own_rows, tile)
        return carry

    lax.fori_loop(0, model // tile, pick, 0)

    def exchange(src, dst, send_sem, recv_sem):
        for i, (dy, dx) in enumerate(moves):
            there = plane(dy, dx)
            send(remote(src.at[there], dst.at[e], send_sem.at[i], recv_sem.at[i], (there, f)))
        return pltpu.make_async_copy(src.at[e], dst.at[e], local_sem.at[7])

    def arrivals(dst, send_sem, recv_sem):
        for i, (dy, dx) in enumerate(moves):
            src = plane(SIDE - dy, SIDE - dx)
            remote(dst.at[src], dst.at[src], send_sem.at[i], recv_sem.at[i], (src, f)).wait_recv()

    own = exchange(outgoing, received, go_send, go_recv)
    own.start()

    def shared(step, carry):
        cols = pl.ds(pl.multiple_of(step * tile, tile), tile)
        value = jnp.dot(shared_hidden, sdown[:, cols], preferred_element_type=F32)
        partial[:, :, cols] = value.reshape(n_f, own_rows, tile)
        return carry

    lax.fori_loop(0, model // tile, shared, 0)
    for copy in weight_copies[3:]:
        copy.wait()
    own.wait()
    arrivals(received, go_send, go_recv)

    def inner(step, carry):
        cols = pl.ds(pl.multiple_of(step * tile, tile), tile)
        x = received[...].reshape(slots, model)
        gate_proj = jnp.dot(x, gate[:, cols], preferred_element_type=F32)
        up_proj = jnp.dot(x, up[:, cols], preferred_element_type=F32)
        hidden[:, cols] = (jax.nn.silu(gate_proj) * up_proj).astype(BF16)
        return carry

    lax.fori_loop(0, hid // tile, inner, 0)

    def outer(step, carry):
        cols = pl.ds(pl.multiple_of(step * tile, tile), tile)
        value = jnp.dot(hidden[...], down[:, cols], preferred_element_type=F32)
        served[:, :, cols] = value.astype(BF16).reshape(n_e, own_rows, tile)
        return carry

    lax.fori_loop(0, model // tile, outer, 0)
    own = exchange(served, returned, back_send, back_recv)
    own.start()
    own.wait()
    arrivals(returned, back_send, back_recv)

    def share(step, carry):
        cols = pl.ds(pl.multiple_of(step * tile, tile), tile)
        back = returned[:, :, cols].reshape(slots, tile)
        value = partial[:, :, cols].reshape(rows, tile)
        for i in range(2):
            value = value + jnp.dot(combine[i], back, preferred_element_type=F32)
        value = value.reshape(n_f, own_rows, tile)
        partial[:, :, cols] = value
        parts_out[:, :, cols] = value.astype(BF16)
        return carry

    lax.fori_loop(0, model // tile, share, 0)
    incoming = []
    for i in range(1, n_f):
        there = column(i)
        copy = remote(
            parts_out.at[there], parts_in.at[i - 1], part_send.at[i - 1], part_recv.at[i - 1], (e, there)
        )
        send(copy)
        incoming.append(copy)
    value = partial[f]
    for i, copy in enumerate(incoming):
        copy.wait_recv()
        value = value + parts_in[i].astype(F32)
    out_ref[...] = value.astype(BF16)
    for copy in sent:
        copy.wait_send()


def moe(tokens, meta, expert_gate, expert_up, expert_down, shared_gate, shared_up, shared_down):
    n_e, n_f = lax.axis_size("expert"), lax.axis_size("feat")
    own_rows, lanes = meta.shape
    model = tokens.shape[1]
    hid = expert_gate.shape[2]
    slots = n_e * own_rows
    vmem = pl.BlockSpec(memory_space=pltpu.VMEM)
    hbm = pl.BlockSpec(memory_space=pl.ANY)
    dma = pltpu.SemaphoreType.DMA
    weights = (expert_gate[0], expert_up[0], expert_down[0], shared_gate, shared_up, shared_down)
    return pl.pallas_call(
        moe_kernel,
        name="moe",
        out_shape=jax.ShapeDtypeStruct((own_rows, model), BF16),
        in_specs=[vmem, vmem] + [hbm] * 6,
        out_specs=vmem,
        scratch_shapes=[pltpu.VMEM(w.shape, BF16) for w in weights]
        + [
            pltpu.VMEM((n_f, own_rows, lanes), F32),
            pltpu.VMEM((n_f, own_rows, model), F32),
            pltpu.VMEM((2, n_f * own_rows, slots), BF16),
            pltpu.VMEM((n_e, own_rows, model), BF16),
            pltpu.VMEM((n_e, own_rows, model), BF16),
            pltpu.VMEM((slots, hid), BF16),
            pltpu.VMEM((n_e, own_rows, model), BF16),
            pltpu.VMEM((n_e, own_rows, model), BF16),
            pltpu.VMEM((n_f, own_rows, model), BF16),
            pltpu.VMEM((n_f - 1, own_rows, model), BF16),
            dma((8,)),
            dma((n_f - 1,)),
            dma((n_f - 1,)),
            dma((n_e - 1,)),
            dma((n_e - 1,)),
            dma((n_e - 1,)),
            dma((n_e - 1,)),
            dma((n_f - 1,)),
            dma((n_f - 1,)),
        ],
        compiler_params=pltpu.CompilerParams(
            collective_id=1, has_side_effects=True, vmem_limit_bytes=60 * 1024 * 1024
        ),
    )(tokens, meta, expert_gate, expert_up, expert_down, shared_gate, shared_up, shared_down)


def shards(
    tokens,
    expert_ids,
    gate_weights,
    expert_gate,
    expert_up,
    expert_down,
    shared_gate,
    shared_up,
    shared_down,
    encoder,
    encoder_bias,
    decoder,
    decoder_bias,
):
    meta = jnp.concatenate([expert_ids.astype(F32), gate_weights], axis=1)
    meta = jnp.pad(meta, ((0, 0), (0, 128 - meta.shape[1])))
    rows = moe(tokens, meta, expert_gate, expert_up, expert_down, shared_gate, shared_up, shared_down)
    return sae(rows, encoder, encoder_bias, decoder, decoder_bias)


def solution(mesh):
    return jax.shard_map(
        shards,
        mesh=mesh,
        in_specs=(
            P("expert", None),
            P(("expert", "feat"), None),
            P(("expert", "feat"), None),
            P(("expert", "feat"), None, None),
            P(("expert", "feat"), None, None),
            P(("expert", "feat"), None, None),
            P(None, "feat"),
            P(None, "feat"),
            P("feat", None),
            P(None, ("expert", "feat")),
            P(("expert", "feat")),
            P(("expert", "feat"), None),
            P(),
        ),
        out_specs=(P(None, ("expert", "feat")), P(("expert", "feat"), None)),
        check_vma=False,
    )
```

```python
import jax
import jax.numpy as jnp
from jax import lax
from jax.experimental import pallas as pl
from jax.experimental.pallas import tpu as pltpu
from jax.sharding import PartitionSpec as P

MESH = pl.DeviceIdType.MESH
SIDE = 4
ORDERS = ((1, 0, 2), (0, 2, 1), (2, 1, 0))
PARTS = len(ORDERS)
ALL = slice(None)
BF16 = jnp.bfloat16
F32 = jnp.float32
OUTWARD = (0, 1, -1, 2)
INWARD = (2, 1, -1, 0)
FAR_WAY = {0: 1, 2: 1, 1: -1, -1: -1}
FAR, MINUS, PLUS = 0, 1, 2
OTHERS = (1, -1, 2)
TOP = 8
COPIES = 18


class Torus:
    def __init__(self):
        self.e, self.f = lax.axis_index("expert"), lax.axis_index("feat")
        self.core = lax.rem(self.f, 2)
        self.other = 1 - self.core
        self.pos = (self.e // SIDE, lax.rem(self.e, SIDE), self.f // 2)
        self.partner = (self.e, self.f + 1 - 2 * self.core)

    def at(self, axis, delta):
        return lax.rem(self.pos[axis] + delta + SIDE, SIDE) if delta else self.pos[axis]

    def device(self, axis, delta):
        there = list(self.pos)
        there[axis] = self.at(axis, delta)
        return (there[0] * SIDE + there[1], there[2] * 2 + self.core)

    def index(self, part, offsets):
        idx = [None] * 3
        for axis, delta in zip(ORDERS[part], offsets):
            idx[axis] = ALL if delta is None else self.at(axis, delta)
        return tuple(idx)

    def meet(self, peers):
        barrier = pltpu.get_barrier_semaphore()
        for there in peers:
            pl.semaphore_signal(barrier, inc=1, device_id=there, device_id_type=MESH)
        pl.semaphore_wait(barrier, len(peers))


def remote(src, dst, send, recv, where):
    return pltpu.make_async_remote_copy(
        src_ref=src, dst_ref=dst, send_sem=send, recv_sem=recv, device_id=where, device_id_type=MESH
    )


class Gather:
    def __init__(self, torus, buf, send, recv):
        self.torus, self.buf, self.send, self.recv = torus, buf, send, recv
        self.specs = [(0, d, (0, 0, 0), (-d, 0, 0)) for d in OTHERS]
        self.specs += [(1, d, (None, 0, 0), (None, -d, 0)) for d in OTHERS]
        for d in OUTWARD:
            way = FAR_WAY[d]
            self.specs += [
                (2, 1, (None, d, 0), (None, d, -1)),
                (2, -1, (None, d, 0), (None, d, 1)),
                (2, way, (None, d, -way), (None, d, 2)),
            ]
        self.started = []

    def cells(self, part, offsets):
        return self.buf.at[(part, *self.torus.index(part, offsets))]

    def copy(self, part, k, landing):
        slot, delta, source, target = self.specs[k]
        cells = self.cells(part, target if landing else source)
        return remote(
            cells, cells, self.send.at[part, k], self.recv.at[part, k], self.torus.device(ORDERS[part][slot], delta)
        )

    def start(self, part, *ks):
        for k in ks:
            copy = self.copy(part, k, False)
            copy.start()
            self.started.append(copy)

    def wait(self, part, *ks):
        for k in ks:
            self.copy(part, k, True).wait_recv()

    def run(self, arrived):
        parts = range(PARTS)
        plane = {d: 6 + 3 * i for i, d in enumerate(OUTWARD)}
        for p in parts:
            self.wait(p, 0, 1, 2)
            self.start(p, 3, 4, 5)
        for p in parts:
            self.start(p, plane[0], plane[0] + 1)
        for i, d in enumerate((-1, 1, 2)):
            for p in parts:
                self.wait(p, 3 + i)
                self.start(p, plane[d], plane[d] + 1)
            if d == 1:
                for p in parts:
                    self.wait(p, plane[0], plane[0] + 1)
                    self.start(p, plane[0] + 2)
        for p in parts:
            arrived(p, 0)
        for d in (-1, 1, 2):
            for p in parts:
                self.wait(p, plane[d], plane[d] + 1)
                self.start(p, plane[d] + 2)
        for p in parts:
            arrived(p, -1)
            arrived(p, 1)
        for p in parts:
            for d in OUTWARD:
                self.wait(p, plane[d] + 2)
            arrived(p, 2)

    def drain(self):
        for copy in self.started:
            copy.wait_send()


class Scatter:
    def __init__(self, torus, total, planes, lines, blocks, send, recv):
        self.torus, self.total, self.send, self.recv = torus, total, send, recv
        self.specs = []
        for i, d in enumerate(INWARD):
            for way, last, kind in ((FAR_WAY[d], 2, FAR), (1, 1, MINUS), (-1, -1, PLUS)):
                self.specs.append((2, way, (None, d, last), planes, (kind, i)))
        self.specs += [(1, d, (None, d, 0), lines, (i,)) for i, d in enumerate(INWARD[:3])]
        self.specs += [(0, d, (d, 0, 0), blocks, (i,)) for i, d in enumerate(INWARD[:3])]
        self.started = []

    def cells(self, part, offsets):
        return (part, *self.torus.index(part, offsets))

    def copy(self, part, k):
        slot, delta, source, lands, place = self.specs[k]
        return remote(
            self.total.at[self.cells(part, source)],
            lands.at[(part, *place)],
            self.send.at[part, k],
            self.recv.at[part, k],
            self.torus.device(ORDERS[part][slot], delta),
        )

    def start(self, part, *ks):
        for k in ks:
            copy = self.copy(part, k)
            copy.start()
            self.started.append(copy)

    def landed(self, part, k):
        self.copy(part, k).wait_recv()
        _, _, _, lands, place = self.specs[k]
        return lands[(part, *place)].astype(F32)

    def add(self, part, offsets, ks):
        idx = self.cells(part, offsets)
        value = self.total[idx].astype(F32)
        for k in ks:
            value = value + self.landed(part, k)
        return idx, value

    def run(self, produce, finish):
        parts = range(PARTS)
        plane = {d: 3 * i for i, d in enumerate(INWARD)}

        def raw(p, way):
            for d in INWARD:
                if FAR_WAY[d] != way:
                    self.start(p, plane[d] + (1 if way == 1 else 2))

        for p in parts:
            produce(p, 2)
            self.start(p, *(plane[d] for d in INWARD))
        for p in parts:
            produce(p, 1)
            raw(p, 1)
            produce(p, -1)
            raw(p, -1)
        for p in parts:
            produce(p, 0)
        for d in INWARD:
            way = FAR_WAY[d]
            for p in parts:
                idx, value = self.add(p, (None, d, way), (plane[d],))
                self.total[idx] = value.astype(BF16)
                self.start(p, plane[d] + (1 if way == 1 else 2))
        for i, d in enumerate(INWARD):
            for p in parts:
                idx, value = self.add(p, (None, d, 0), (plane[d] + 1, plane[d] + 2))
                self.total[idx] = value.astype(BF16)
                if d:
                    self.start(p, 12 + i)
        for p in parts:
            idx, value = self.add(p, (None, 0, 0), (12, 13, 14))
            self.total[idx] = value.astype(BF16)
            self.start(p, 15, 16, 17)
        for p in parts:
            _, value = self.add(p, (0, 0, 0), (15, 16, 17))
            finish(p, value)

    def drain(self):
        for copy in self.started:
            copy.wait_send()


MOVES = (
    (2, 2), (1, 2), (3, 2), (2, 1), (2, 3), (0, 2), (2, 0), (1, 1),
    (1, 3), (3, 1), (3, 3), (0, 1), (0, 3), (1, 0), (3, 0), (0, 0),
)
HALF = len(MOVES) // 2
TILE = 256


def tiles(size, body):
    def step(i, carry):
        body(pl.ds(pl.multiple_of(i * TILE, TILE), TILE))
        return carry

    lax.fori_loop(0, size // TILE, step, 0)


def layer_kernel(
    tokens_ref, ids_ref, weights_ref, gate_hbm, up_hbm, down_hbm, sgate_hbm, sup_hbm, sdown_hbm,
    enc_hbm, bias_ref, dec_hbm, feat_hbm, rec_ref,
    gate, up, down, sgate, sup, sdown, meta, metas, partial, combine, outgoing, received, hidden, served, returned,
    parts_out, parts_in, gathered, total, planes, lines, blocks, scores, feats, enc, dec, bias,
    local_sem, meta_send, meta_recv, go_send, go_recv, back_send, back_recv, part_send, part_recv,
    ag_send, ag_recv, rs_send, rs_recv, cross_send, cross_recv,
):
    torus = Torus()
    e, f, core, other, partner = torus.e, torus.f, torus.core, torus.other, torus.partner
    n_e, own_rows, model = outgoing.shape
    n_f = metas.shape[0]
    rows = n_f * own_rows
    slots = n_e * own_rows
    chunk = HALF * own_rows
    width = gathered.shape[-1]
    features = enc.shape[2]

    weight_copies = [
        pltpu.make_async_copy(src, dst, local_sem.at[i])
        for i, (src, dst) in enumerate(
            (
                (sgate_hbm, sgate), (sup_hbm, sup), (sdown_hbm, sdown),
                (gate_hbm.at[0], gate), (up_hbm.at[0], up), (down_hbm.at[0], down),
                (enc_hbm, enc.at[core]), (bias_ref, bias.at[core]), (dec_hbm, dec.at[core]),
            )
        )
    ]
    for copy in weight_copies:
        copy.start()
    own_sem, feat_sem = local_sem.at[9], local_sem.at[10]

    meta[...] = jnp.zeros_like(meta)
    meta[:TOP, :own_rows] = ids_ref[...].astype(F32)
    meta[TOP:, :own_rows] = weights_ref[...]
    metas[f] = meta[...]

    def plane(move, sign=1):
        dy, dx = move
        y = lax.rem(torus.pos[0] + SIDE + sign * dy, SIDE)
        return y * SIDE + lax.rem(torus.pos[1] + SIDE + sign * dx, SIDE)

    def column(i):
        return lax.rem(f + i, n_f)

    torus.meet(
        [(plane(m), f) for m in MOVES[:-1]]
        + [(e, column(i)) for i in range(1, n_f)]
    )
    sent = []

    def send(copy):
        copy.start()
        sent.append(copy)

    for i in range(1, n_f):
        send(remote(meta, metas.at[f], meta_send.at[i - 1], meta_recv.at[i - 1], (e, column(i))))

    for copy in weight_copies[:3]:
        copy.wait()
    tokens = tokens_ref[...]
    shared_gate = jnp.dot(tokens, sgate[...], preferred_element_type=F32)
    shared_up = jnp.dot(tokens, sup[...], preferred_element_type=F32)
    shared_hidden = (jax.nn.silu(shared_gate) * shared_up).astype(BF16)

    for i in range(1, n_f):
        src = column(n_f - i)
        remote(metas.at[src], metas.at[src], meta_send.at[i - 1], meta_recv.at[i - 1], (e, src)).wait_recv()
    turned = metas[...].reshape(rows, metas.shape[2]).T[:own_rows]
    table = jnp.concatenate(
        [turned] + [pltpu.roll(turned, rows - own_rows * i, 1) for i in range(1, n_f)], axis=0
    )
    slot = lax.broadcasted_iota(jnp.int32, (rows, slots), 1)
    token = lax.broadcasted_iota(jnp.int32, (rows, slots), 0)
    column_slot = lax.broadcasted_iota(jnp.int32, (1, slots), 1) // own_rows
    wanted = jnp.zeros((1, slots), jnp.int32)
    for i, move in enumerate(MOVES):
        wanted = jnp.where(column_slot == i, plane(move) * n_f + f, wanted)
    wanted = wanted.astype(F32)
    named = jnp.zeros((rows, slots), F32)
    weight = jnp.zeros((rows, slots), F32)
    for k in range(TOP):
        same = table[:, k : k + 1] == wanted
        named = named + jnp.where(same, 1.0, 0.0)
        weight = weight + jnp.where(same, table[:, TOP + k : TOP + k + 1], 0.0)
    row = lax.broadcasted_iota(jnp.int32, (rows, rows), 0)
    col = lax.broadcasted_iota(jnp.int32, (rows, rows), 1)
    before = jnp.where((row // own_rows == col // own_rows) & (col < row), 1.0, 0.0).astype(BF16)
    rank = jnp.dot(before, named.astype(BF16), preferred_element_type=F32)
    here = (lax.rem(slot, 2).astype(F32) == rank) & (lax.rem(slot // 2, n_f) == token // own_rows)
    places = jnp.where(here, named, 0.0)
    weight = places * weight
    high = weight.astype(BF16)
    combine[0] = high
    combine[1] = (weight - high.astype(F32)).astype(BF16)
    dispatch = places.T.astype(BF16)

    halves = (range(HALF), range(HALF, n_e))

    def span(half):
        return slice(half * HALF, (half + 1) * HALF)

    def exchange(src, dst, send_sem, recv_sem, half):
        for i in halves[half]:
            if i < n_e - 1:
                send(remote(src.at[i], dst.at[i], send_sem.at[i], recv_sem.at[i], (plane(MOVES[i]), f)))
            else:
                copy = pltpu.make_async_copy(src.at[i], dst.at[i], own_sem)
                copy.start()

    def arrivals(src, dst, send_sem, recv_sem, half):
        for i in halves[half]:
            if i < n_e - 1:
                remote(
                    src.at[i], dst.at[i], send_sem.at[i], recv_sem.at[i], (plane(MOVES[i], -1), f)
                ).wait_recv()
            else:
                pltpu.make_async_copy(src.at[i], dst.at[i], own_sem).wait()

    for half in range(2):
        mine = dispatch[half * chunk : (half + 1) * chunk]

        def pick(cols, half=half, mine=mine):
            value = jnp.dot(mine, tokens_ref[:, cols], preferred_element_type=F32)
            outgoing[span(half), :, cols] = value.astype(BF16).reshape(HALF, own_rows, TILE)

        tiles(model, pick)
        exchange(outgoing, received, go_send, go_recv, half)

    for copy in weight_copies[6:]:
        copy.wait()
    cross_copies = [
        remote(ref.at[core], ref.at[core], cross_send.at[i], cross_recv.at[i], partner)
        for i, ref in enumerate((enc, bias, dec))
    ]
    for copy in cross_copies:
        send(copy)

    def shared(cols):
        value = jnp.dot(shared_hidden, sdown[:, cols], preferred_element_type=F32)
        partial[:, :, cols] = value.reshape(n_f, own_rows, TILE)

    tiles(model, shared)
    for copy in weight_copies[3:6]:
        copy.wait()

    for half in range(2):
        arrivals(outgoing, received, go_send, go_recv, half)

        def inner(cols, half=half):
            x = received[span(half)].reshape(chunk, model)
            gate_proj = jnp.dot(x, gate[:, cols], preferred_element_type=F32)
            up_proj = jnp.dot(x, up[:, cols], preferred_element_type=F32)
            hidden[:, cols] = (jax.nn.silu(gate_proj) * up_proj).astype(BF16)

        tiles(hidden.shape[1], inner)

        def outer(cols, half=half):
            value = jnp.dot(hidden[...], down[:, cols], preferred_element_type=F32)
            served[span(half), :, cols] = value.astype(BF16).reshape(HALF, own_rows, TILE)

        tiles(model, outer)
        for i in halves[half]:
            if i < n_e - 1:
                send(
                    remote(
                        served.at[i], returned.at[i], back_send.at[i], back_recv.at[i], (plane(MOVES[i], -1), f)
                    )
                )
            else:
                pltpu.make_async_copy(served.at[i], returned.at[i], own_sem).start()

    def summed(cols, half):
        back = returned[span(half), :, cols].reshape(chunk, TILE)
        value = partial[:, :, cols].reshape(rows, TILE)
        for i in range(2):
            value = value + jnp.dot(
                combine[i, :, half * chunk : (half + 1) * chunk], back, preferred_element_type=F32
            )
        value = value.reshape(n_f, own_rows, TILE)
        partial[:, :, cols] = value
        return value

    def returns(half):
        for i in halves[half]:
            if i < n_e - 1:
                remote(
                    served.at[i], returned.at[i], back_send.at[i], back_recv.at[i], (plane(MOVES[i]), f)
                ).wait_recv()
            else:
                pltpu.make_async_copy(served.at[i], returned.at[i], own_sem).wait()

    def fill(y, carry):
        for which in range(2):
            scores[which, y] = jnp.broadcast_to(bias[which], (SIDE, SIDE, own_rows, features))
        return carry

    for copy in cross_copies:
        copy.wait_recv()
    lax.fori_loop(0, SIDE, fill, 0)

    def share_far(cols):
        summed(cols, 0)

    returns(0)
    tiles(model, share_far)
    returns(1)
    incoming = {}
    for p in range(PARTS):

        def share_near(i, carry, p=p):
            cols = pl.ds(pl.multiple_of(p * width + i * TILE, TILE), TILE)
            parts_out[:, :, cols] = summed(cols, 1).astype(BF16)
            return carry

        lax.fori_loop(0, width // TILE, share_near, 0)
        cols = pl.ds(p * width, width)
        for i in range(1, n_f):
            there = column(i)
            copy = remote(
                parts_out.at[there, :, cols], parts_in.at[i - 1, :, cols],
                part_send.at[p, i - 1], part_recv.at[p, i - 1], (e, there),
            )
            send(copy)
            incoming[p, i] = copy

    gather = Gather(torus, gathered, ag_send, ag_recv)
    for p in range(PARTS):
        cols = pl.ds(p * width, width)
        value = partial[f, :, cols]
        for i in range(1, n_f):
            incoming[p, i].wait_recv()
            value = value + parts_in[i - 1, :, cols].astype(F32)
        gathered[(p, *torus.pos)] = value.astype(BF16)
        gather.start(p, 0, 1, 2)

    def encode(p, delta):
        idx = torus.index(p, (None, None, delta))

        def step(i, carry):
            which = i // (features // TILE)
            cols = pl.ds(pl.multiple_of(lax.rem(i, features // TILE) * TILE, TILE), TILE)
            block = gathered[(p, *idx)].reshape(SIDE * SIDE * own_rows, width)
            value = jnp.dot(block, enc[which, p * width : (p + 1) * width, cols], preferred_element_type=F32)
            at = (which, *idx, ALL, cols)
            scores[at] = scores[at] + value.reshape(SIDE, SIDE, own_rows, TILE)
            return carry

        lax.fori_loop(0, 2 * features // TILE, step, 0)

    gather.run(encode)

    def rectify(y, carry):
        for which in range(2):
            feats[which, y] = jnp.maximum(scores[which, y], 0.0).astype(BF16)
        return carry

    lax.fori_loop(0, SIDE, rectify, 0)
    own_out = pltpu.make_async_copy(feats.at[core], feat_hbm.at[:, :, :, core], feat_sem)
    cross_out = remote(
        feats.at[other], feat_hbm.at[:, :, :, core], cross_send.at[3], cross_recv.at[3], partner
    )
    cross_in = remote(
        feats.at[other], feat_hbm.at[:, :, :, other], cross_send.at[3], cross_recv.at[3], partner
    )
    own_out.start()
    cross_out.start()

    scatter = Scatter(torus, total, planes, lines, blocks, rs_send, rs_recv)

    def produce(p, delta):
        idx = torus.index(p, (None, None, delta))
        left = [feats[(which, *idx)].reshape(SIDE * SIDE * own_rows, features) for which in range(2)]

        def step(i, carry):
            cols = pl.ds(pl.multiple_of(i * TILE, TILE), TILE)
            here = pl.ds(pl.multiple_of(p * width + i * TILE, TILE), TILE)
            value = jnp.dot(left[0], dec[0, :, here], preferred_element_type=F32) + jnp.dot(
                left[1], dec[1, :, here], preferred_element_type=F32
            )
            total[(p, *idx, ALL, cols)] = value.astype(BF16).reshape(SIDE, SIDE, own_rows, TILE)
            return carry

        lax.fori_loop(0, width // TILE, step, 0)

    def finish(p, value):
        rec_ref[:, p * width : (p + 1) * width] = value

    scatter.run(produce, finish)

    own_out.wait()
    cross_out.wait_send()
    cross_in.wait_recv()
    for copy in sent:
        copy.wait_send()
    gather.drain()
    scatter.drain()


def layer(tokens, ids, weights, routed, shared, encoder, encoder_bias, decoder):
    n_e, n_f = lax.axis_size("expert"), lax.axis_size("feat")
    own_rows = ids.shape[1]
    model = tokens.shape[1]
    hid = routed[0].shape[2]
    slots = n_e * own_rows
    rows = n_f * own_rows
    features = encoder.shape[1]
    width = model // PARTS
    cube = (SIDE, SIDE, SIDE)
    vmem = pl.BlockSpec(memory_space=pltpu.VMEM)
    hbm = pl.BlockSpec(memory_space=pl.ANY)
    dma = pltpu.SemaphoreType.DMA
    plane_rows = pltpu.VMEM((n_e, own_rows, model), BF16)
    torus_sem = dma((PARTS, COPIES))
    return pl.pallas_call(
        layer_kernel,
        name="layer",
        out_shape=(
            jax.ShapeDtypeStruct((*cube, 2, own_rows, features), BF16),
            jax.ShapeDtypeStruct((own_rows, model), F32),
        ),
        in_specs=[vmem] * 3 + [hbm] * 7 + [vmem, hbm],
        out_specs=(hbm, vmem),
        scratch_shapes=[pltpu.VMEM(w.shape[1:], BF16) for w in routed]
        + [pltpu.VMEM(w.shape, BF16) for w in shared]
        + [
            pltpu.VMEM((2 * TOP, rows), F32),
            pltpu.VMEM((n_f, 2 * TOP, rows), F32),
            pltpu.VMEM((n_f, own_rows, model), F32),
            pltpu.VMEM((2, rows, slots), BF16),
            plane_rows,
            plane_rows,
            pltpu.VMEM((HALF * own_rows, hid), BF16),
            plane_rows,
            plane_rows,
            pltpu.VMEM((n_f, own_rows, model), BF16),
            pltpu.VMEM((n_f - 1, own_rows, model), BF16),
            pltpu.VMEM((PARTS, *cube, own_rows, width), BF16),
            pltpu.VMEM((PARTS, *cube, own_rows, width), BF16),
            pltpu.VMEM((PARTS, 3, SIDE, SIDE, own_rows, width), BF16),
            pltpu.VMEM((PARTS, 3, SIDE, own_rows, width), BF16),
            pltpu.VMEM((PARTS, 3, own_rows, width), BF16),
            pltpu.VMEM((2, *cube, own_rows, features), F32),
            pltpu.VMEM((2, *cube, own_rows, features), BF16),
            pltpu.VMEM((2, model, features), BF16),
            pltpu.VMEM((2, features, model), BF16),
            pltpu.VMEM((2, 1, features), F32),
            dma((11,)),
            dma((n_f - 1,)),
            dma((n_f - 1,)),
            dma((n_e - 1,)),
            dma((n_e - 1,)),
            dma((n_e - 1,)),
            dma((n_e - 1,)),
            dma((PARTS, n_f - 1)),
            dma((PARTS, n_f - 1)),
            torus_sem, torus_sem, torus_sem, torus_sem,
            dma((4,)),
            dma((4,)),
        ],
        compiler_params=pltpu.CompilerParams(
            collective_id=0, has_side_effects=True, vmem_limit_bytes=63 * 1024 * 1024
        ),
    )(tokens, ids, weights, *routed, *shared, encoder, encoder_bias, decoder)


def shards(
    tokens,
    expert_ids,
    gate_weights,
    expert_gate,
    expert_up,
    expert_down,
    shared_gate,
    shared_up,
    shared_down,
    encoder,
    encoder_bias,
    decoder,
    decoder_bias,
):
    features, sums = layer(
        tokens,
        expert_ids.T,
        gate_weights.T,
        (expert_gate, expert_up, expert_down),
        (shared_gate, shared_up, shared_down),
        encoder,
        encoder_bias[None, :],
        decoder,
    )
    return features.reshape(-1, encoder.shape[1]), sums + decoder_bias[None, :]


def solution(mesh):
    return jax.shard_map(
        shards,
        mesh=mesh,
        in_specs=(
            P("expert", None),
            P(("expert", "feat"), None),
            P(("expert", "feat"), None),
            P(("expert", "feat"), None, None),
            P(("expert", "feat"), None, None),
            P(("expert", "feat"), None, None),
            P(None, "feat"),
            P(None, "feat"),
            P("feat", None),
            P(None, ("expert", "feat")),
            P(("expert", "feat")),
            P(("expert", "feat"), None),
            P(),
        ),
        out_specs=(P(None, ("expert", "feat")), P(("expert", "feat"), None)),
        check_vma=False,
    )
```

```python
import functools

import jax
import jax.numpy as jnp
from jax import lax
from jax.experimental import pallas as pl
from jax.experimental.pallas import tpu as pltpu
from jax.sharding import PartitionSpec as P

MESH = pl.DeviceIdType.MESH
SIDE = 4
ORDERS = ((1, 0, 2), (0, 2, 1), (2, 1, 0))
PARTS = len(ORDERS)
ALL = slice(None)
BF16 = jnp.bfloat16
F32 = jnp.float32
OUTWARD = (0, 1, -1, 2)
INWARD = (2, 1, -1, 0)
FAR_WAY = {0: 1, 2: 1, 1: -1, -1: -1}
FAR, MINUS, PLUS = 0, 1, 2
OTHERS = (1, -1, 2)
TOP = 8
COPIES = 18


class Torus:
    def __init__(self):
        self.e, self.f = lax.axis_index("expert"), lax.axis_index("feat")
        self.core = lax.rem(self.f, 2)
        self.other = 1 - self.core
        self.pos = (self.e // SIDE, lax.rem(self.e, SIDE), self.f // 2)
        self.partner = (self.e, self.f + 1 - 2 * self.core)

    def at(self, axis, delta):
        return lax.rem(self.pos[axis] + delta + SIDE, SIDE) if delta else self.pos[axis]

    def device(self, axis, delta):
        there = list(self.pos)
        there[axis] = self.at(axis, delta)
        return (there[0] * SIDE + there[1], there[2] * 2 + self.core)

    def index(self, part, offsets):
        idx = [None] * 3
        for axis, delta in zip(ORDERS[part], offsets):
            idx[axis] = ALL if delta is None else self.at(axis, delta)
        return tuple(idx)

    def meet(self, peers):
        barrier = pltpu.get_barrier_semaphore()
        for there in peers:
            pl.semaphore_signal(barrier, inc=1, device_id=there, device_id_type=MESH)
        pl.semaphore_wait(barrier, len(peers))


def remote(src, dst, send, recv, where):
    return pltpu.make_async_remote_copy(
        src_ref=src, dst_ref=dst, send_sem=send, recv_sem=recv, device_id=where, device_id_type=MESH
    )


class Gather:
    def __init__(self, torus, buf, send, recv):
        self.torus, self.buf, self.send, self.recv = torus, buf, send, recv
        self.specs = [(0, d, (0, 0, 0), (-d, 0, 0)) for d in OTHERS]
        self.specs += [(1, d, (None, 0, 0), (None, -d, 0)) for d in OTHERS]
        for d in OUTWARD:
            way = FAR_WAY[d]
            self.specs += [
                (2, 1, (None, d, 0), (None, d, -1)),
                (2, -1, (None, d, 0), (None, d, 1)),
                (2, way, (None, d, -way), (None, d, 2)),
            ]
        self.started = []

    def cells(self, part, offsets):
        return self.buf.at[(part, *self.torus.index(part, offsets))]

    def copy(self, part, k, landing):
        slot, delta, source, target = self.specs[k]
        cells = self.cells(part, target if landing else source)
        return remote(
            cells, cells, self.send.at[part, k], self.recv.at[part, k], self.torus.device(ORDERS[part][slot], delta)
        )

    def start(self, part, *ks):
        for k in ks:
            copy = self.copy(part, k, False)
            copy.start()
            self.started.append(copy)

    def wait(self, part, *ks):
        for k in ks:
            self.copy(part, k, True).wait_recv()

    def steps(self, p, arrived):
        plane = {d: 6 + 3 * i for i, d in enumerate(OUTWARD)}

        def go_on(d):
            self.wait(p, plane[d], plane[d] + 1)
            self.start(p, plane[d] + 2)

        def lines():
            self.wait(p, 0, 1, 2)
            self.start(p, 3, 4, 5, plane[0], plane[0] + 1)

        def near_planes():
            for k, d in ((3, -1), (4, 1)):
                self.wait(p, k)
                self.start(p, plane[d], plane[d] + 1)
            go_on(0)

        def far_planes():
            self.wait(p, 5)
            self.start(p, plane[2], plane[2] + 1)
            arrived(p, 0)

        def far_near():
            go_on(-1)
            go_on(1)
            go_on(2)

        def last():
            arrived(p, -1)
            arrived(p, 1)
            self.wait(p, *(plane[d] + 2 for d in OUTWARD))
            arrived(p, 2)

        return lines, near_planes, far_planes, far_near, last

    def drain(self):
        for copy in self.started:
            copy.wait_send()


class Scatter:
    def __init__(self, torus, total, planes, lines, blocks, send, recv):
        self.torus, self.total, self.send, self.recv = torus, total, send, recv
        self.specs = []
        for i, d in enumerate(INWARD):
            for way, last, kind in ((FAR_WAY[d], 2, FAR), (1, 1, MINUS), (-1, -1, PLUS)):
                self.specs.append((2, way, (None, d, last), planes, (kind, i)))
        self.specs += [(1, d, (None, d, 0), lines, (i,)) for i, d in enumerate(INWARD[:3])]
        self.specs += [(0, d, (d, 0, 0), blocks, (i,)) for i, d in enumerate(INWARD[:3])]
        self.started = []

    def cells(self, part, offsets):
        return (part, *self.torus.index(part, offsets))

    def copy(self, part, k):
        slot, delta, source, lands, place = self.specs[k]
        return remote(
            self.total.at[self.cells(part, source)],
            lands.at[(part, *place)],
            self.send.at[part, k],
            self.recv.at[part, k],
            self.torus.device(ORDERS[part][slot], delta),
        )

    def start(self, part, *ks):
        for k in ks:
            copy = self.copy(part, k)
            copy.start()
            self.started.append(copy)

    def landed(self, part, k):
        self.copy(part, k).wait_recv()
        _, _, _, lands, place = self.specs[k]
        return lands[(part, *place)].astype(F32)

    def add(self, part, offsets, ks):
        idx = self.cells(part, offsets)
        value = self.total[idx].astype(F32)
        for k in ks:
            value = value + self.landed(part, k)
        return idx, value

    def run(self, produce, finish):
        parts = range(PARTS)
        plane = {d: 3 * i for i, d in enumerate(INWARD)}

        def raw(p, way):
            for d in INWARD:
                if FAR_WAY[d] != way:
                    self.start(p, plane[d] + (1 if way == 1 else 2))

        for p in parts:
            produce(p, 2)
            self.start(p, *(plane[d] for d in INWARD))
        for p in parts:
            produce(p, 1)
            raw(p, 1)
            produce(p, -1)
            raw(p, -1)
        for p in parts:
            produce(p, 0)
        for d in INWARD:
            way = FAR_WAY[d]
            for p in parts:
                idx, value = self.add(p, (None, d, way), (plane[d],))
                self.total[idx] = value.astype(BF16)
                self.start(p, plane[d] + (1 if way == 1 else 2))
        for i, d in enumerate(INWARD):
            for p in parts:
                idx, value = self.add(p, (None, d, 0), (plane[d] + 1, plane[d] + 2))
                self.total[idx] = value.astype(BF16)
                if d:
                    self.start(p, 12 + i)
        for p in parts:
            idx, value = self.add(p, (None, 0, 0), (12, 13, 14))
            self.total[idx] = value.astype(BF16)
            self.start(p, 15, 16, 17)
        for p in parts:
            _, value = self.add(p, (0, 0, 0), (15, 16, 17))
            finish(p, value)

    def drain(self):
        for copy in self.started:
            copy.wait_send()


MOVES = (
    (2, 2), (1, 2), (3, 2), (2, 1), (2, 3), (0, 2), (2, 0), (1, 1),
    (1, 3), (3, 1), (3, 3), (0, 1), (0, 3), (1, 0), (3, 0), (0, 0),
)
HALF = len(MOVES) // 2
TILE = 256


def tiles(size, body):
    def step(i, carry):
        body(pl.ds(pl.multiple_of(i * TILE, TILE), TILE))
        return carry

    lax.fori_loop(0, size // TILE, step, 0)


def layer_kernel(
    tokens_ref, ids_ref, weights_ref, gate_hbm, up_hbm, down_hbm, sgate_hbm, sup_hbm, sdown_hbm,
    enc_hbm, bias_ref, dec_hbm, feat_hbm, rec_ref,
    gate, up, down, sgate, sup, sdown, meta, metas, partial, combine, outgoing, received, hidden, served, returned,
    parts_out, parts_in, gathered, total, planes, lines, blocks, scores, feats, enc, dec, bias,
    local_sem, meta_send, meta_recv, go_send, go_recv, back_send, back_recv, part_send, part_recv,
    ag_send, ag_recv, rs_send, rs_recv, cross_send, cross_recv,
):
    torus = Torus()
    e, f, core, other, partner = torus.e, torus.f, torus.core, torus.other, torus.partner
    n_e, own_rows, model = outgoing.shape
    n_f = metas.shape[0]
    rows = n_f * own_rows
    slots = n_e * own_rows
    chunk = HALF * own_rows
    width = gathered.shape[-1]
    features = enc.shape[2]

    weight_copies = [
        pltpu.make_async_copy(src, dst, local_sem.at[i])
        for i, (src, dst) in enumerate(
            (
                (sgate_hbm, sgate), (sup_hbm, sup), (sdown_hbm, sdown),
                (gate_hbm.at[0], gate), (up_hbm.at[0], up), (down_hbm.at[0], down),
                (enc_hbm, enc.at[core]), (bias_ref, bias.at[core]), (dec_hbm, dec.at[core]),
            )
        )
    ]
    for copy in weight_copies:
        copy.start()
    feat_sem = local_sem.at[9]

    meta[...] = jnp.zeros_like(meta)
    meta[:TOP, :own_rows] = ids_ref[...].astype(F32)
    meta[TOP:, :own_rows] = weights_ref[...]
    metas[f] = meta[...]

    def plane(move, sign=1):
        dy, dx = move
        y = lax.rem(torus.pos[0] + SIDE + sign * dy, SIDE)
        return y * SIDE + lax.rem(torus.pos[1] + SIDE + sign * dx, SIDE)

    def column(i):
        return lax.rem(f + i, n_f)

    torus.meet(
        [(plane(m), f) for m in MOVES[:-1]]
        + [(e, column(i)) for i in range(1, n_f)]
    )
    sent = []

    def send(copy):
        copy.start()
        sent.append(copy)

    for i in range(1, n_f):
        send(remote(meta, metas.at[f], meta_send.at[i - 1], meta_recv.at[i - 1], (e, column(i))))

    for copy in weight_copies[:3]:
        copy.wait()
    tokens = tokens_ref[...]
    shared_gate = jnp.dot(tokens, sgate[...], preferred_element_type=F32)
    shared_up = jnp.dot(tokens, sup[...], preferred_element_type=F32)
    shared_hidden = (jax.nn.silu(shared_gate) * shared_up).astype(BF16)

    for i in range(1, n_f):
        src = column(n_f - i)
        remote(metas.at[src], metas.at[src], meta_send.at[i - 1], meta_recv.at[i - 1], (e, src)).wait_recv()
    turned = metas[...].reshape(rows, metas.shape[2]).T[:own_rows]
    table = jnp.concatenate(
        [turned] + [pltpu.roll(turned, rows - own_rows * i, 1) for i in range(1, n_f)], axis=0
    )
    slot = lax.broadcasted_iota(jnp.int32, (rows, slots), 1)
    token = lax.broadcasted_iota(jnp.int32, (rows, slots), 0)
    column_slot = lax.broadcasted_iota(jnp.int32, (1, slots), 1) // own_rows
    wanted = jnp.zeros((1, slots), jnp.int32)
    for i, move in enumerate(MOVES):
        wanted = jnp.where(column_slot == i, plane(move) * n_f + f, wanted)
    wanted = wanted.astype(F32)
    named = jnp.zeros((rows, slots), F32)
    weight = jnp.zeros((rows, slots), F32)
    for k in range(TOP):
        same = table[:, k : k + 1] == wanted
        named = named + jnp.where(same, 1.0, 0.0)
        weight = weight + jnp.where(same, table[:, TOP + k : TOP + k + 1], 0.0)
    row = lax.broadcasted_iota(jnp.int32, (rows, rows), 0)
    col = lax.broadcasted_iota(jnp.int32, (rows, rows), 1)
    before = jnp.where((row // own_rows == col // own_rows) & (col < row), 1.0, 0.0).astype(BF16)
    rank = jnp.dot(before, named.astype(BF16), preferred_element_type=F32)
    here = (lax.rem(slot, 2).astype(F32) == rank) & (lax.rem(slot // 2, n_f) == token // own_rows)
    places = jnp.where(here, named, 0.0)
    weight = places * weight
    high = weight.astype(BF16)
    combine[0] = high
    combine[1] = (weight - high.astype(F32)).astype(BF16)
    dispatch = places.T.astype(BF16)

    halves = (range(HALF), range(HALF, n_e - 1))

    def span(half):
        return slice(half * HALF, (half + 1) * HALF)

    for half in range(2):
        mine = dispatch[half * chunk : (half + 1) * chunk]

        def pick(cols, half=half, mine=mine):
            value = jnp.dot(mine, tokens_ref[:, cols], preferred_element_type=F32)
            value = value.astype(BF16).reshape(HALF, own_rows, TILE)
            outgoing[span(half), :, cols] = value
            if half:
                received[n_e - 1, :, cols] = value[HALF - 1]

        tiles(model, pick)
        for i in halves[half]:
            send(remote(outgoing.at[i], received.at[i], go_send.at[i], go_recv.at[i], (plane(MOVES[i]), f)))

    for copy in weight_copies[6:]:
        copy.wait()
    cross_copies = [
        remote(ref.at[core], ref.at[core], cross_send.at[i], cross_recv.at[i], partner)
        for i, ref in enumerate((enc, bias, dec))
    ]
    for copy in cross_copies:
        send(copy)

    def shared(cols):
        value = jnp.dot(shared_hidden, sdown[:, cols], preferred_element_type=F32)
        partial[:, :, cols] = value.reshape(n_f, own_rows, TILE)

    tiles(model, shared)
    for copy in weight_copies[3:6]:
        copy.wait()

    for half in range(2):
        for i in halves[half]:
            remote(
                outgoing.at[i], received.at[i], go_send.at[i], go_recv.at[i], (plane(MOVES[i], -1), f)
            ).wait_recv()

        def inner(cols, half=half):
            x = received[span(half)].reshape(chunk, model)
            gate_proj = jnp.dot(x, gate[:, cols], preferred_element_type=F32)
            up_proj = jnp.dot(x, up[:, cols], preferred_element_type=F32)
            hidden[half, :, cols] = (jax.nn.silu(gate_proj) * up_proj).astype(BF16)

        tiles(hidden.shape[2], inner)

    def part_tiles(p, body):
        def step(i, carry):
            body(pl.ds(pl.multiple_of(p * width + i * TILE, TILE), TILE))
            return carry

        lax.fori_loop(0, width // TILE, step, 0)

    def back_copy(p, i, sign):
        cols = pl.ds(p * width, width)
        return remote(
            served.at[i, :, cols], returned.at[i, :, cols],
            back_send.at[p, i], back_recv.at[p, i], (plane(MOVES[i], sign), f),
        )

    def outer(cols):
        value = jnp.dot(hidden[...].reshape(slots, hidden.shape[2]), down[:, cols], preferred_element_type=F32)
        value = value.astype(BF16).reshape(n_e, own_rows, TILE)
        served[:, :, cols] = value
        returned[n_e - 1, :, cols] = value[n_e - 1]

    for p in range(PARTS):
        part_tiles(p, outer)
        for i in range(n_e - 1):
            send(back_copy(p, i, -1))

    def fill(y, carry):
        for which in range(2):
            scores[which, y] = jnp.broadcast_to(bias[which], (SIDE, SIDE, own_rows, features))
        return carry

    for copy in cross_copies:
        copy.wait_recv()
    lax.fori_loop(0, SIDE, fill, 0)

    gather = Gather(torus, gathered, ag_send, ag_recv)
    incoming = {}

    def share(cols):
        back = returned[:, :, cols].reshape(slots, TILE)
        value = partial[:, :, cols].reshape(rows, TILE)
        for i in range(2):
            value = value + jnp.dot(combine[i], back, preferred_element_type=F32)
        value = value.reshape(n_f, own_rows, TILE)
        partial[:, :, cols] = value
        parts_out[:, :, cols] = value.astype(BF16)

    def give(p):
        for i in range(n_e - 1):
            back_copy(p, i, 1).wait_recv()
        part_tiles(p, share)
        cols = pl.ds(p * width, width)
        for i in range(1, n_f):
            there = column(i)
            copy = remote(
                parts_out.at[there, :, cols], parts_in.at[i - 1, :, cols],
                part_send.at[p, i - 1], part_recv.at[p, i - 1], (e, there),
            )
            send(copy)
            incoming[p, i] = copy

    def take(p):
        cols = pl.ds(p * width, width)
        value = partial[f, :, cols]
        for i in range(1, n_f):
            incoming[p, i].wait_recv()
            value = value + parts_in[i - 1, :, cols].astype(F32)
        gathered[(p, *torus.pos)] = value.astype(BF16)
        gather.start(p, 0, 1, 2)

    def encode(p, delta):
        idx = torus.index(p, (None, None, delta))

        def step(i, carry):
            which = i // (features // TILE)
            cols = pl.ds(pl.multiple_of(lax.rem(i, features // TILE) * TILE, TILE), TILE)
            block = gathered[(p, *idx)].reshape(SIDE * SIDE * own_rows, width)
            value = jnp.dot(block, enc[which, p * width : (p + 1) * width, cols], preferred_element_type=F32)
            at = (which, *idx, ALL, cols)
            scores[at] = scores[at] + value.reshape(SIDE, SIDE, own_rows, TILE)
            return carry

        lax.fori_loop(0, 2 * features // TILE, step, 0)

    steps = [
        [functools.partial(give, p), functools.partial(take, p), *gather.steps(p, encode)] for p in range(PARTS)
    ]
    for turn in range(len(steps[0]) + PARTS - 1):
        for p in reversed(range(PARTS)):
            if 0 <= turn - p < len(steps[p]):
                steps[p][turn - p]()

    def rectify(y, carry):
        for which in range(2):
            feats[which, y] = jnp.maximum(scores[which, y], 0.0).astype(BF16)
        return carry

    lax.fori_loop(0, SIDE, rectify, 0)
    own_out = pltpu.make_async_copy(feats.at[core], feat_hbm.at[:, :, :, core], feat_sem)
    cross_out = remote(
        feats.at[other], feat_hbm.at[:, :, :, core], cross_send.at[3], cross_recv.at[3], partner
    )
    cross_in = remote(
        feats.at[other], feat_hbm.at[:, :, :, other], cross_send.at[3], cross_recv.at[3], partner
    )
    own_out.start()
    cross_out.start()

    scatter = Scatter(torus, total, planes, lines, blocks, rs_send, rs_recv)

    def produce(p, delta):
        idx = torus.index(p, (None, None, delta))
        left = [feats[(which, *idx)].reshape(SIDE * SIDE * own_rows, features) for which in range(2)]

        def step(i, carry):
            cols = pl.ds(pl.multiple_of(i * TILE, TILE), TILE)
            here = pl.ds(pl.multiple_of(p * width + i * TILE, TILE), TILE)
            value = jnp.dot(left[0], dec[0, :, here], preferred_element_type=F32) + jnp.dot(
                left[1], dec[1, :, here], preferred_element_type=F32
            )
            total[(p, *idx, ALL, cols)] = value.astype(BF16).reshape(SIDE, SIDE, own_rows, TILE)
            return carry

        lax.fori_loop(0, width // TILE, step, 0)

    def finish(p, value):
        rec_ref[:, p * width : (p + 1) * width] = value

    scatter.run(produce, finish)

    own_out.wait()
    cross_out.wait_send()
    cross_in.wait_recv()
    for copy in sent:
        copy.wait_send()
    gather.drain()
    scatter.drain()


def layer(tokens, ids, weights, routed, shared, encoder, encoder_bias, decoder):
    n_e, n_f = lax.axis_size("expert"), lax.axis_size("feat")
    own_rows = ids.shape[1]
    model = tokens.shape[1]
    hid = routed[0].shape[2]
    slots = n_e * own_rows
    rows = n_f * own_rows
    features = encoder.shape[1]
    width = model // PARTS
    cube = (SIDE, SIDE, SIDE)
    vmem = pl.BlockSpec(memory_space=pltpu.VMEM)
    hbm = pl.BlockSpec(memory_space=pl.ANY)
    dma = pltpu.SemaphoreType.DMA
    plane_rows = pltpu.VMEM((n_e, own_rows, model), BF16)
    torus_sem = dma((PARTS, COPIES))
    return pl.pallas_call(
        layer_kernel,
        name="layer",
        out_shape=(
            jax.ShapeDtypeStruct((*cube, 2, own_rows, features), BF16),
            jax.ShapeDtypeStruct((own_rows, model), F32),
        ),
        in_specs=[vmem] * 3 + [hbm] * 7 + [vmem, hbm],
        out_specs=(hbm, vmem),
        scratch_shapes=[pltpu.VMEM(w.shape[1:], BF16) for w in routed]
        + [pltpu.VMEM(w.shape, BF16) for w in shared]
        + [
            pltpu.VMEM((2 * TOP, rows), F32),
            pltpu.VMEM((n_f, 2 * TOP, rows), F32),
            pltpu.VMEM((n_f, own_rows, model), F32),
            pltpu.VMEM((2, rows, slots), BF16),
            plane_rows,
            plane_rows,
            pltpu.VMEM((2, HALF * own_rows, hid), BF16),
            plane_rows,
            plane_rows,
            pltpu.VMEM((n_f, own_rows, model), BF16),
            pltpu.VMEM((n_f - 1, own_rows, model), BF16),
            pltpu.VMEM((PARTS, *cube, own_rows, width), BF16),
            pltpu.VMEM((PARTS, *cube, own_rows, width), BF16),
            pltpu.VMEM((PARTS, 3, SIDE, SIDE, own_rows, width), BF16),
            pltpu.VMEM((PARTS, 3, SIDE, own_rows, width), BF16),
            pltpu.VMEM((PARTS, 3, own_rows, width), BF16),
            pltpu.VMEM((2, *cube, own_rows, features), F32),
            pltpu.VMEM((2, *cube, own_rows, features), BF16),
            pltpu.VMEM((2, model, features), BF16),
            pltpu.VMEM((2, features, model), BF16),
            pltpu.VMEM((2, 1, features), F32),
            dma((10,)),
            dma((n_f - 1,)),
            dma((n_f - 1,)),
            dma((n_e - 1,)),
            dma((n_e - 1,)),
            dma((PARTS, n_e - 1)),
            dma((PARTS, n_e - 1)),
            dma((PARTS, n_f - 1)),
            dma((PARTS, n_f - 1)),
            torus_sem, torus_sem, torus_sem, torus_sem,
            dma((4,)),
            dma((4,)),
        ],
        compiler_params=pltpu.CompilerParams(
            collective_id=0, has_side_effects=True, vmem_limit_bytes=63 * 1024 * 1024
        ),
    )(tokens, ids, weights, *routed, *shared, encoder, encoder_bias, decoder)


def finish_kernel(feat_hbm, sums_ref, bias_ref, out_hbm, rec_ref, held, in_sem, out_sem):
    reads = [pltpu.make_async_copy(feat_hbm.at[y], held.at[y], in_sem.at[y]) for y in range(SIDE)]
    writes = [pltpu.make_async_copy(held.at[y], out_hbm.at[y], out_sem.at[y]) for y in range(SIDE)]
    for copy in reads:
        copy.start()
    lanes = bias_ref.shape[1]
    for i in range(bias_ref.shape[0]):
        cols = slice(i * lanes, (i + 1) * lanes)
        rec_ref[:, cols] = sums_ref[:, cols] + bias_ref[i : i + 1, :]
    for y in range(SIDE):
        reads[y].wait()
        writes[y].start()
    for copy in writes:
        copy.wait()


def finish(features, sums, bias):
    vmem = pl.BlockSpec(memory_space=pltpu.VMEM)
    hbm = pl.BlockSpec(memory_space=pl.ANY)
    return pl.pallas_call(
        finish_kernel,
        name="finish",
        out_shape=(
            jax.ShapeDtypeStruct(features.shape, features.dtype),
            jax.ShapeDtypeStruct(sums.shape, sums.dtype),
        ),
        in_specs=[hbm, vmem, vmem],
        out_specs=(hbm, vmem),
        scratch_shapes=[
            pltpu.VMEM(features.shape, features.dtype),
            pltpu.SemaphoreType.DMA((SIDE,)),
            pltpu.SemaphoreType.DMA((SIDE,)),
        ],
        compiler_params=pltpu.CompilerParams(vmem_limit_bytes=60 * 1024 * 1024),
    )(features, sums, bias.reshape(-1, 128))


def shards(
    tokens,
    expert_ids,
    gate_weights,
    expert_gate,
    expert_up,
    expert_down,
    shared_gate,
    shared_up,
    shared_down,
    encoder,
    encoder_bias,
    decoder,
    decoder_bias,
):
    features, sums = layer(
        tokens,
        expert_ids.T,
        gate_weights.T,
        (expert_gate, expert_up, expert_down),
        (shared_gate, shared_up, shared_down),
        encoder,
        encoder_bias[None, :],
        decoder,
    )
    features, sums = finish(features, sums, decoder_bias)
    return features.reshape(-1, encoder.shape[1]), sums


def solution(mesh):
    return jax.shard_map(
        shards,
        mesh=mesh,
        in_specs=(
            P("expert", None),
            P(("expert", "feat"), None),
            P(("expert", "feat"), None),
            P(("expert", "feat"), None, None),
            P(("expert", "feat"), None, None),
            P(("expert", "feat"), None, None),
            P(None, "feat"),
            P(None, "feat"),
            P("feat", None),
            P(None, ("expert", "feat")),
            P(("expert", "feat")),
            P(("expert", "feat"), None),
            P(),
        ),
        out_specs=(P(None, ("expert", "feat")), P(("expert", "feat"), None)),
        check_vma=False,
    )
```

```python
import functools

import jax
import jax.numpy as jnp
from jax import lax
from jax.experimental import pallas as pl
from jax.experimental.pallas import tpu as pltpu
from jax.sharding import PartitionSpec as P

MESH = pl.DeviceIdType.MESH
SIDE = 4
ORDERS = ((1, 0, 2), (0, 2, 1), (2, 1, 0))
PARTS = len(ORDERS)
ALL = slice(None)
BF16 = jnp.bfloat16
F32 = jnp.float32
OUTWARD = (0, 1, -1, 2)
INWARD = (2, 1, -1, 0)
FAR_WAY = {0: 1, 2: 1, 1: -1, -1: -1}
FAR, MINUS, PLUS = 0, 1, 2
OTHERS = (1, -1, 2)
TOP = 8
COPIES = 18


class Torus:
    def __init__(self):
        self.e, self.f = lax.axis_index("expert"), lax.axis_index("feat")
        self.core = lax.rem(self.f, 2)
        self.other = 1 - self.core
        self.pos = (self.e // SIDE, lax.rem(self.e, SIDE), self.f // 2)
        self.partner = (self.e, self.f + 1 - 2 * self.core)

    def at(self, axis, delta):
        return lax.rem(self.pos[axis] + delta + SIDE, SIDE) if delta else self.pos[axis]

    def device(self, axis, delta):
        there = list(self.pos)
        there[axis] = self.at(axis, delta)
        return (there[0] * SIDE + there[1], there[2] * 2 + self.core)

    def index(self, part, offsets):
        idx = [None] * 3
        for axis, delta in zip(ORDERS[part], offsets):
            idx[axis] = ALL if delta is None else self.at(axis, delta)
        return tuple(idx)

    def meet(self, peers):
        barrier = pltpu.get_barrier_semaphore()
        for there in peers:
            pl.semaphore_signal(barrier, inc=1, device_id=there, device_id_type=MESH)
        pl.semaphore_wait(barrier, len(peers))


def remote(src, dst, send, recv, where):
    return pltpu.make_async_remote_copy(
        src_ref=src, dst_ref=dst, send_sem=send, recv_sem=recv, device_id=where, device_id_type=MESH
    )


class Gather:
    def __init__(self, torus, buf, send, recv):
        self.torus, self.buf, self.send, self.recv = torus, buf, send, recv
        self.specs = [(0, d, (0, 0, 0), (-d, 0, 0)) for d in OTHERS]
        self.specs += [(1, d, (None, 0, 0), (None, -d, 0)) for d in OTHERS]
        for d in OUTWARD:
            way = FAR_WAY[d]
            self.specs += [
                (2, 1, (None, d, 0), (None, d, -1)),
                (2, -1, (None, d, 0), (None, d, 1)),
                (2, way, (None, d, -way), (None, d, 2)),
            ]
        self.started = []

    def cells(self, part, offsets):
        return self.buf.at[(part, *self.torus.index(part, offsets))]

    def copy(self, part, k, landing):
        slot, delta, source, target = self.specs[k]
        cells = self.cells(part, target if landing else source)
        return remote(
            cells, cells, self.send.at[part, k], self.recv.at[part, k], self.torus.device(ORDERS[part][slot], delta)
        )

    def start(self, part, *ks):
        for k in ks:
            copy = self.copy(part, k, False)
            copy.start()
            self.started.append(copy)

    def wait(self, part, *ks):
        for k in ks:
            self.copy(part, k, True).wait_recv()

    def steps(self, p):
        plane = {d: 6 + 3 * i for i, d in enumerate(OUTWARD)}

        def go_on(d):
            self.wait(p, plane[d], plane[d] + 1)
            self.start(p, plane[d] + 2)

        def lines():
            self.wait(p, 0, 1, 2)
            self.start(p, 3, 4, 5, plane[0], plane[0] + 1)

        def near_planes():
            for k, d in ((3, -1), (4, 1)):
                self.wait(p, k)
                self.start(p, plane[d], plane[d] + 1)
            go_on(0)

        def far_planes():
            self.wait(p, 5)
            self.start(p, plane[2], plane[2] + 1)

        def far_arrivals():
            self.wait(p, *(plane[d] + 2 for d in OUTWARD))

        return lines, near_planes, far_planes, [functools.partial(go_on, d) for d in (-1, 1, 2)], far_arrivals

    def drain(self):
        for copy in self.started:
            copy.wait_send()


class Scatter:
    def __init__(self, torus, total, planes, lines, blocks, send, recv):
        self.torus, self.total, self.send, self.recv = torus, total, send, recv
        self.specs = []
        for i, d in enumerate(INWARD):
            for way, last, kind in ((FAR_WAY[d], 2, FAR), (1, 1, MINUS), (-1, -1, PLUS)):
                self.specs.append((2, way, (None, d, last), planes, (kind, i)))
        self.specs += [(1, d, (None, d, 0), lines, (i,)) for i, d in enumerate(INWARD[:3])]
        self.specs += [(0, d, (d, 0, 0), blocks, (i,)) for i, d in enumerate(INWARD[:3])]
        self.started = []

    def cells(self, part, offsets):
        return (part, *self.torus.index(part, offsets))

    def copy(self, part, k):
        slot, delta, source, lands, place = self.specs[k]
        return remote(
            self.total.at[self.cells(part, source)],
            lands.at[(part, *place)],
            self.send.at[part, k],
            self.recv.at[part, k],
            self.torus.device(ORDERS[part][slot], delta),
        )

    def start(self, part, *ks):
        for k in ks:
            copy = self.copy(part, k)
            copy.start()
            self.started.append(copy)

    def landed(self, part, k):
        self.copy(part, k).wait_recv()
        _, _, _, lands, place = self.specs[k]
        return lands[(part, *place)].astype(F32)

    def add(self, part, offsets, ks):
        idx = self.cells(part, offsets)
        value = self.total[idx].astype(F32)
        for k in ks:
            value = value + self.landed(part, k)
        return idx, value

    def run(self, produce, finish):
        parts = range(PARTS)
        plane = {d: 3 * i for i, d in enumerate(INWARD)}

        def raw(p, way):
            for d in INWARD:
                if FAR_WAY[d] != way:
                    self.start(p, plane[d] + (1 if way == 1 else 2))

        for p in parts:
            produce(p, 2)
            self.start(p, *(plane[d] for d in INWARD))
        for p in parts:
            produce(p, 1)
            raw(p, 1)
            produce(p, -1)
            raw(p, -1)
        for d in INWARD:
            way = FAR_WAY[d]
            for p in parts:
                idx, value = self.add(p, (None, d, way), (plane[d],))
                self.total[idx] = value.astype(BF16)
                self.start(p, plane[d] + (1 if way == 1 else 2))
        for p in parts:
            produce(p, 0)
        for i, d in enumerate(INWARD):
            for p in parts:
                idx, value = self.add(p, (None, d, 0), (plane[d] + 1, plane[d] + 2))
                self.total[idx] = value.astype(BF16)
                if d:
                    self.start(p, 12 + i)
        for p in parts:
            idx, value = self.add(p, (None, 0, 0), (12, 13, 14))
            self.total[idx] = value.astype(BF16)
            self.start(p, 15, 16, 17)
        for p in parts:
            _, value = self.add(p, (0, 0, 0), (15, 16, 17))
            finish(p, value)

    def drain(self):
        for copy in self.started:
            copy.wait_send()


MOVES = (
    (2, 2), (1, 2), (3, 2), (2, 1), (2, 3), (0, 2), (2, 0), (1, 1),
    (1, 3), (3, 1), (3, 3), (0, 1), (0, 3), (1, 0), (3, 0), (0, 0),
)
HALF = len(MOVES) // 2
TILE = 768
HIDDEN_TILE = 512


def tiles(size, body, tile=TILE):
    def step(i, carry):
        body(pl.ds(pl.multiple_of(i * tile, tile), tile))
        return carry

    lax.fori_loop(0, size // tile, step, 0)


def layer_kernel(
    tokens_hbm, ids_ref, weights_ref, gate_hbm, up_hbm, down_hbm, sgate_hbm, sup_hbm, sdown_hbm,
    enc_hbm, bias_ref, dec_hbm, feat_hbm, rec_ref,
    gate, up, down, sgate, sup, sdown, meta, metas, partial, combine, outgoing, received, hidden, served, returned,
    parts_out, parts_in, gathered, total, planes, lines, blocks, scores, feats, enc, dec, bias,
    tokens_ref, local_sem, meta_send, meta_recv, go_send, go_recv, back_send, back_recv, part_send, part_recv,
    ag_send, ag_recv, rs_send, rs_recv, cross_send, cross_recv,
):
    torus = Torus()
    e, f, core, other, partner = torus.e, torus.f, torus.core, torus.other, torus.partner
    n_e, own_rows, model = outgoing.shape
    n_f = metas.shape[0]
    rows = n_f * own_rows
    slots = n_e * own_rows
    chunk = HALF * own_rows
    width = gathered.shape[-1]
    features = enc.shape[2]

    weight_copies = [
        pltpu.make_async_copy(src, dst, local_sem.at[i])
        for i, (src, dst) in enumerate(
            (
                (sgate_hbm, sgate), (sup_hbm, sup), (sdown_hbm, sdown),
                (gate_hbm.at[0], gate), (up_hbm.at[0], up), (down_hbm.at[0], down),
                (enc_hbm, enc.at[core]), (bias_ref, bias.at[core]), (dec_hbm, dec.at[core]),
            )
        )
    ]
    tokens_copy = pltpu.make_async_copy(tokens_hbm, tokens_ref, local_sem.at[10])
    feat_sem = local_sem.at[9]

    meta[...] = jnp.zeros_like(meta)
    meta[:TOP, :own_rows] = ids_ref[...].astype(F32)
    meta[TOP:, :own_rows] = weights_ref[...]
    metas[f] = meta[...]
    for copy in [tokens_copy] + weight_copies:
        copy.start()

    def plane(move, sign=1):
        dy, dx = move
        y = lax.rem(torus.pos[0] + SIDE + sign * dy, SIDE)
        return y * SIDE + lax.rem(torus.pos[1] + SIDE + sign * dx, SIDE)

    def column(i):
        return lax.rem(f + i, n_f)

    torus.meet(
        [(plane(m), f) for m in MOVES[:-1]]
        + [(e, column(i)) for i in range(1, n_f)]
    )
    sent = []

    def send(copy):
        copy.start()
        sent.append(copy)

    for i in range(1, n_f):
        send(remote(meta, metas.at[f], meta_send.at[i - 1], meta_recv.at[i - 1], (e, column(i))))

    for copy in weight_copies[:3]:
        copy.wait()
    tokens_copy.wait()
    tokens = tokens_ref[...]
    shared_gate = jnp.dot(tokens, sgate[...], preferred_element_type=F32)
    shared_up = jnp.dot(tokens, sup[...], preferred_element_type=F32)
    shared_hidden = (jax.nn.silu(shared_gate) * shared_up).astype(BF16)

    for i in range(1, n_f):
        src = column(n_f - i)
        remote(metas.at[src], metas.at[src], meta_send.at[i - 1], meta_recv.at[i - 1], (e, src)).wait_recv()
    turned = metas[...].reshape(rows, metas.shape[2]).T[:own_rows]
    table = jnp.concatenate(
        [turned] + [pltpu.roll(turned, rows - own_rows * i, 1) for i in range(1, n_f)], axis=0
    )
    slot = lax.broadcasted_iota(jnp.int32, (rows, slots), 1)
    token = lax.broadcasted_iota(jnp.int32, (rows, slots), 0)
    column_slot = lax.broadcasted_iota(jnp.int32, (1, slots), 1) // own_rows
    wanted = jnp.zeros((1, slots), jnp.int32)
    for i, move in enumerate(MOVES):
        wanted = jnp.where(column_slot == i, plane(move) * n_f + f, wanted)
    wanted = wanted.astype(F32)
    named = jnp.zeros((rows, slots), F32)
    weight = jnp.zeros((rows, slots), F32)
    for k in range(TOP):
        same = table[:, k : k + 1] == wanted
        named = named + jnp.where(same, 1.0, 0.0)
        weight = weight + jnp.where(same, table[:, TOP + k : TOP + k + 1], 0.0)
    row = lax.broadcasted_iota(jnp.int32, (rows, rows), 0)
    col = lax.broadcasted_iota(jnp.int32, (rows, rows), 1)
    before = jnp.where((row // own_rows == col // own_rows) & (col < row), 1.0, 0.0).astype(BF16)
    rank = jnp.dot(before, named.astype(BF16), preferred_element_type=F32)
    here = (lax.rem(slot, 2).astype(F32) == rank) & (lax.rem(slot // 2, n_f) == token // own_rows)
    places = jnp.where(here, named, 0.0)
    weight = places * weight
    high = weight.astype(BF16)
    combine[0] = high
    combine[1] = (weight - high.astype(F32)).astype(BF16)
    dispatch = places.T.astype(BF16)

    halves = (range(HALF), range(HALF, n_e - 1))

    def span(half):
        return slice(half * HALF, (half + 1) * HALF)

    for half in range(2):
        mine = dispatch[half * chunk : (half + 1) * chunk]

        def pick(cols, half=half, mine=mine):
            value = jnp.dot(mine, tokens_ref[:, cols], preferred_element_type=F32)
            value = value.astype(BF16).reshape(HALF, own_rows, TILE)
            outgoing[span(half), :, cols] = value
            if half:
                received[n_e - 1, :, cols] = value[HALF - 1]

        tiles(model, pick)
        for i in halves[half]:
            send(remote(outgoing.at[i], received.at[i], go_send.at[i], go_recv.at[i], (plane(MOVES[i]), f)))

    for copy in weight_copies[6:]:
        copy.wait()
    cross_copies = [
        remote(ref.at[core], ref.at[core], cross_send.at[i], cross_recv.at[i], partner)
        for i, ref in enumerate((enc, bias, dec))
    ]
    for copy in cross_copies:
        send(copy)

    def shared(cols):
        value = jnp.dot(shared_hidden, sdown[:, cols], preferred_element_type=F32)
        partial[:, :, cols] = value.reshape(n_f, own_rows, TILE)

    tiles(model, shared)
    for copy in weight_copies[3:6]:
        copy.wait()

    for half in range(2):
        for i in halves[half]:
            remote(
                outgoing.at[i], received.at[i], go_send.at[i], go_recv.at[i], (plane(MOVES[i], -1), f)
            ).wait_recv()

        def inner(cols, half=half):
            x = received[span(half)].reshape(chunk, model)
            gate_proj = jnp.dot(x, gate[:, cols], preferred_element_type=F32)
            up_proj = jnp.dot(x, up[:, cols], preferred_element_type=F32)
            hidden[half, :, cols] = (jax.nn.silu(gate_proj) * up_proj).astype(BF16)

        tiles(hidden.shape[2], inner, HIDDEN_TILE)

    def back_copy(p, i, sign):
        cols = pl.ds(p * width, width)
        return remote(
            served.at[i, :, cols], returned.at[i, :, cols],
            back_send.at[p, i], back_recv.at[p, i], (plane(MOVES[i], sign), f),
        )

    def outer(cols):
        value = jnp.dot(hidden[...].reshape(slots, hidden.shape[2]), down[:, cols], preferred_element_type=F32)
        value = value.astype(BF16).reshape(n_e, own_rows, TILE)
        served[:, :, cols] = value
        returned[n_e - 1, :, cols] = value[n_e - 1]

    for p in range(PARTS):
        outer(pl.ds(p * width, width))
        for i in range(n_e - 1):
            send(back_copy(p, i, -1))

    def fill(y, carry):
        for which in range(2):
            scores[which, y] = jnp.broadcast_to(bias[which], (SIDE, SIDE, own_rows, features))
        return carry

    for copy in cross_copies:
        copy.wait_recv()
    lax.fori_loop(0, SIDE, fill, 0)

    gather = Gather(torus, gathered, ag_send, ag_recv)
    incoming = {}

    def share(cols):
        back = returned[:, :, cols].reshape(slots, TILE)
        value = partial[:, :, cols].reshape(rows, TILE)
        for i in range(2):
            value = value + jnp.dot(combine[i], back, preferred_element_type=F32)
        value = value.reshape(n_f, own_rows, TILE)
        partial[:, :, cols] = value
        parts_out[:, :, cols] = value.astype(BF16)

    def give(p):
        for i in range(n_e - 1):
            back_copy(p, i, 1).wait_recv()
        cols = pl.ds(p * width, width)
        share(cols)
        for i in range(1, n_f):
            there = column(i)
            copy = remote(
                parts_out.at[there, :, cols], parts_in.at[i - 1, :, cols],
                part_send.at[p, i - 1], part_recv.at[p, i - 1], (e, there),
            )
            send(copy)
            incoming[p, i] = copy

    def take(p):
        cols = pl.ds(p * width, width)
        value = partial[f, :, cols]
        for i in range(1, n_f):
            incoming[p, i].wait_recv()
            value = value + parts_in[i - 1, :, cols].astype(F32)
        gathered[(p, *torus.pos)] = value.astype(BF16)
        gather.start(p, 0, 1, 2)

    def encode(p, delta):
        idx = torus.index(p, (None, None, delta))

        block = gathered[(p, *idx)].reshape(SIDE * SIDE * own_rows, width)
        for which in range(2):
            value = jnp.dot(block, enc[which, p * width : (p + 1) * width, :], preferred_element_type=F32)
            at = (which, *idx)
            scores[at] = scores[at] + value.reshape(SIDE, SIDE, own_rows, features)

    steps = [gather.steps(p) for p in range(PARTS)]
    early = [
        [functools.partial(give, p), functools.partial(take, p), *steps[p][:3]] for p in range(PARTS)
    ]
    for turn in range(len(early[0]) + PARTS - 1):
        for p in reversed(range(PARTS)):
            if 0 <= turn - p < len(early[p]):
                early[p][turn - p]()
    for p in range(PARTS):
        encode(p, 0)
    for i in range(3):
        for p in range(PARTS):
            steps[p][3][i]()
    for p in range(PARTS):
        encode(p, -1)
        encode(p, 1)
    for p in range(PARTS):
        steps[p][4]()
        encode(p, 2)

    def rectify(y, carry):
        for which in range(2):
            feats[which, y] = jnp.maximum(scores[which, y], 0.0).astype(BF16)
        return carry

    lax.fori_loop(0, SIDE, rectify, 0)
    own_out = pltpu.make_async_copy(feats.at[core], feat_hbm.at[:, :, :, core], feat_sem)
    cross_out = remote(
        feats.at[other], feat_hbm.at[:, :, :, core], cross_send.at[3], cross_recv.at[3], partner
    )
    cross_in = remote(
        feats.at[other], feat_hbm.at[:, :, :, other], cross_send.at[3], cross_recv.at[3], partner
    )
    own_out.start()
    cross_out.start()

    scatter = Scatter(torus, total, planes, lines, blocks, rs_send, rs_recv)

    def produce(p, delta):
        idx = torus.index(p, (None, None, delta))
        value = 0.0
        for which in range(2):
            block = feats[(which, *idx)].reshape(SIDE * SIDE * own_rows, features)
            value = value + jnp.dot(
                block, dec[which, :, p * width : (p + 1) * width], preferred_element_type=F32
            )
        total[(p, *idx)] = value.astype(BF16).reshape(SIDE, SIDE, own_rows, width)

    def finish(p, value):
        rec_ref[:, p * width : (p + 1) * width] = value

    scatter.run(produce, finish)

    own_out.wait()
    cross_out.wait_send()
    cross_in.wait_recv()
    for copy in sent:
        copy.wait_send()
    gather.drain()
    scatter.drain()


def layer(tokens, ids, weights, routed, shared, encoder, encoder_bias, decoder):
    n_e, n_f = lax.axis_size("expert"), lax.axis_size("feat")
    own_rows = ids.shape[1]
    model = tokens.shape[1]
    hid = routed[0].shape[2]
    slots = n_e * own_rows
    rows = n_f * own_rows
    features = encoder.shape[1]
    width = model // PARTS
    cube = (SIDE, SIDE, SIDE)
    vmem = pl.BlockSpec(memory_space=pltpu.VMEM)
    hbm = pl.BlockSpec(memory_space=pl.ANY)
    dma = pltpu.SemaphoreType.DMA
    plane_rows = pltpu.VMEM((n_e, own_rows, model), BF16)
    torus_sem = dma((PARTS, COPIES))
    return pl.pallas_call(
        layer_kernel,
        name="layer",
        out_shape=(
            jax.ShapeDtypeStruct((*cube, 2, own_rows, features), BF16),
            jax.ShapeDtypeStruct((own_rows, model), F32),
        ),
        in_specs=[hbm] + [vmem] * 2 + [hbm] * 7 + [vmem, hbm],
        out_specs=(hbm, vmem),
        scratch_shapes=[pltpu.VMEM(w.shape[1:], BF16) for w in routed]
        + [pltpu.VMEM(w.shape, BF16) for w in shared]
        + [
            pltpu.VMEM((2 * TOP, rows), F32),
            pltpu.VMEM((n_f, 2 * TOP, rows), F32),
            pltpu.VMEM((n_f, own_rows, model), F32),
            pltpu.VMEM((2, rows, slots), BF16),
            plane_rows,
            plane_rows,
            pltpu.VMEM((2, HALF * own_rows, hid), BF16),
            plane_rows,
            plane_rows,
            pltpu.VMEM((n_f, own_rows, model), BF16),
            pltpu.VMEM((n_f - 1, own_rows, model), BF16),
            pltpu.VMEM((PARTS, *cube, own_rows, width), BF16),
            pltpu.VMEM((PARTS, *cube, own_rows, width), BF16),
            pltpu.VMEM((PARTS, 3, SIDE, SIDE, own_rows, width), BF16),
            pltpu.VMEM((PARTS, 3, SIDE, own_rows, width), BF16),
            pltpu.VMEM((PARTS, 3, own_rows, width), BF16),
            pltpu.VMEM((2, *cube, own_rows, features), F32),
            pltpu.VMEM((2, *cube, own_rows, features), BF16),
            pltpu.VMEM((2, model, features), BF16),
            pltpu.VMEM((2, features, model), BF16),
            pltpu.VMEM((2, 1, features), F32),
            pltpu.VMEM(tokens.shape, BF16),
            dma((11,)),
            dma((n_f - 1,)),
            dma((n_f - 1,)),
            dma((n_e - 1,)),
            dma((n_e - 1,)),
            dma((PARTS, n_e - 1)),
            dma((PARTS, n_e - 1)),
            dma((PARTS, n_f - 1)),
            dma((PARTS, n_f - 1)),
            torus_sem, torus_sem, torus_sem, torus_sem,
            dma((4,)),
            dma((4,)),
        ],
        compiler_params=pltpu.CompilerParams(
            collective_id=0, has_side_effects=True, vmem_limit_bytes=63 * 1024 * 1024
        ),
    )(tokens, ids, weights, *routed, *shared, encoder, encoder_bias, decoder)


def finish_kernel(feat_hbm, sums_hbm, bias_hbm, out_hbm, rec_hbm, held, sums, bias, in_sem, out_sem):
    reads = [
        pltpu.make_async_copy(sums_hbm, sums, in_sem.at[SIDE]),
        pltpu.make_async_copy(bias_hbm, bias, in_sem.at[SIDE + 1]),
    ] + [pltpu.make_async_copy(feat_hbm.at[y], held.at[y], in_sem.at[y]) for y in range(SIDE)]
    writes = [pltpu.make_async_copy(sums, rec_hbm, out_sem.at[SIDE])] + [
        pltpu.make_async_copy(held.at[y], out_hbm.at[y], out_sem.at[y]) for y in range(SIDE)
    ]
    for copy in reads:
        copy.start()
    reads[0].wait()
    reads[1].wait()
    lanes = bias.shape[1]
    for i in range(bias.shape[0]):
        cols = slice(i * lanes, (i + 1) * lanes)
        sums[:, cols] = sums[:, cols] + bias[i : i + 1, :]
    for y in range(SIDE):
        reads[2 + y].wait()
        writes[1 + y].start()
    writes[0].start()
    for copy in writes:
        copy.wait()


def finish(features, sums, bias):
    hbm = pl.BlockSpec(memory_space=pl.ANY)
    bias = bias.reshape(-1, 128)
    return pl.pallas_call(
        finish_kernel,
        name="finish",
        out_shape=(
            jax.ShapeDtypeStruct(features.shape, features.dtype),
            jax.ShapeDtypeStruct(sums.shape, sums.dtype),
        ),
        in_specs=[hbm] * 3,
        out_specs=(hbm, hbm),
        scratch_shapes=[
            pltpu.VMEM(features.shape, features.dtype),
            pltpu.VMEM(sums.shape, sums.dtype),
            pltpu.VMEM(bias.shape, bias.dtype),
            pltpu.SemaphoreType.DMA((SIDE + 2,)),
            pltpu.SemaphoreType.DMA((SIDE + 1,)),
        ],
        compiler_params=pltpu.CompilerParams(vmem_limit_bytes=60 * 1024 * 1024),
    )(features, sums, bias)


def shards(
    tokens,
    expert_ids,
    gate_weights,
    expert_gate,
    expert_up,
    expert_down,
    shared_gate,
    shared_up,
    shared_down,
    encoder,
    encoder_bias,
    decoder,
    decoder_bias,
):
    features, sums = layer(
        tokens,
        expert_ids.T,
        gate_weights.T,
        (expert_gate, expert_up, expert_down),
        (shared_gate, shared_up, shared_down),
        encoder,
        encoder_bias[None, :],
        decoder,
    )
    features, sums = finish(features, sums, decoder_bias)
    return features.reshape(-1, encoder.shape[1]), sums


def solution(mesh):
    return jax.shard_map(
        shards,
        mesh=mesh,
        in_specs=(
            P("expert", None),
            P(("expert", "feat"), None),
            P(("expert", "feat"), None),
            P(("expert", "feat"), None, None),
            P(("expert", "feat"), None, None),
            P(("expert", "feat"), None, None),
            P(None, "feat"),
            P(None, "feat"),
            P("feat", None),
            P(None, ("expert", "feat")),
            P(("expert", "feat")),
            P(("expert", "feat"), None),
            P(),
        ),
        out_specs=(P(None, ("expert", "feat")), P(("expert", "feat"), None)),
        check_vma=False,
    )
```

```python
import functools

import jax
import jax.numpy as jnp
from jax import lax
from jax.experimental import pallas as pl
from jax.experimental.pallas import tpu as pltpu
from jax.sharding import PartitionSpec as P

MESH = pl.DeviceIdType.MESH
SIDE = 4
ORDERS = ((1, 0, 2), (0, 2, 1), (2, 1, 0))
PARTS = len(ORDERS)
ALL = slice(None)
BF16 = jnp.bfloat16
F32 = jnp.float32
OUTWARD = (0, 1, -1, 2)
INWARD = (2, 1, -1, 0)
FAR_WAY = {0: 1, 2: 1, 1: -1, -1: -1}
FAR, MINUS, PLUS = 0, 1, 2
OTHERS = (1, -1, 2)
TOP = 8
COPIES = 18


class Torus:
    def __init__(self):
        self.e, self.f = lax.axis_index("expert"), lax.axis_index("feat")
        self.core = lax.rem(self.f, 2)
        self.other = 1 - self.core
        self.pos = (self.e // SIDE, lax.rem(self.e, SIDE), self.f // 2)
        self.partner = (self.e, self.f + 1 - 2 * self.core)

    def at(self, axis, delta):
        return lax.rem(self.pos[axis] + delta + SIDE, SIDE) if delta else self.pos[axis]

    def device(self, axis, delta):
        there = list(self.pos)
        there[axis] = self.at(axis, delta)
        return (there[0] * SIDE + there[1], there[2] * 2 + self.core)

    def index(self, part, offsets):
        idx = [None] * 3
        for axis, delta in zip(ORDERS[part], offsets):
            idx[axis] = ALL if delta is None else self.at(axis, delta)
        return tuple(idx)


def remote(src, dst, send, recv, where):
    return pltpu.make_async_remote_copy(
        src_ref=src, dst_ref=dst, send_sem=send, recv_sem=recv, device_id=where, device_id_type=MESH
    )


class Gather:
    def __init__(self, torus, bufs, send, recv):
        self.torus, self.bufs, self.send, self.recv = torus, bufs, send, recv
        self.specs = [(0, d, (0, 0, 0), (-d, 0, 0)) for d in OTHERS]
        self.specs += [(1, d, (None, 0, 0), (None, -d, 0)) for d in OTHERS]
        for d in OUTWARD:
            way = FAR_WAY[d]
            self.specs += [
                (2, 1, (None, d, 0), (None, d, -1)),
                (2, -1, (None, d, 0), (None, d, 1)),
                (2, way, (None, d, -way), (None, d, 2)),
            ]
        self.started = []

    def cells(self, part, offsets):
        return self.bufs[part].at[self.torus.index(part, offsets)]

    def copy(self, part, k, landing):
        slot, delta, source, target = self.specs[k]
        cells = self.cells(part, target if landing else source)
        return remote(
            cells, cells, self.send.at[part, k], self.recv.at[part, k], self.torus.device(ORDERS[part][slot], delta)
        )

    def start(self, part, *ks):
        for k in ks:
            copy = self.copy(part, k, False)
            copy.start()
            self.started.append(copy)

    def wait(self, part, *ks):
        for k in ks:
            self.copy(part, k, True).wait_recv()

    def steps(self, p):
        plane = {d: 6 + 3 * i for i, d in enumerate(OUTWARD)}

        def go_on(d):
            self.wait(p, plane[d], plane[d] + 1)
            self.start(p, plane[d] + 2)

        def lines():
            self.wait(p, 0, 1, 2)
            self.start(p, 3, 4, 5, plane[0], plane[0] + 1)

        def near_planes():
            for k, d in ((3, -1), (4, 1)):
                self.wait(p, k)
                self.start(p, plane[d], plane[d] + 1)
            go_on(0)

        def far_planes():
            self.wait(p, 5)
            self.start(p, plane[2], plane[2] + 1)

        def far_arrivals():
            self.wait(p, *(plane[d] + 2 for d in OUTWARD))

        return lines, near_planes, far_planes, [functools.partial(go_on, d) for d in (-1, 1, 2)], far_arrivals

    def drain(self):
        for copy in self.started:
            copy.wait_send()


class Scatter:
    def __init__(self, torus, total, planes, lines, blocks, send, recv):
        self.torus, self.total, self.send, self.recv = torus, total, send, recv
        self.specs = []
        for i, d in enumerate(INWARD):
            for way, last, kind in ((FAR_WAY[d], 2, FAR), (1, 1, MINUS), (-1, -1, PLUS)):
                self.specs.append((2, way, (None, d, last), planes, (kind, i)))
        self.specs += [(1, d, (None, d, 0), lines, (i,)) for i, d in enumerate(INWARD[:3])]
        self.specs += [(0, d, (d, 0, 0), blocks, (i,)) for i, d in enumerate(INWARD[:3])]
        self.started = []

    def cells(self, part, offsets):
        return (part, *self.torus.index(part, offsets))

    def copy(self, part, k):
        slot, delta, source, lands, place = self.specs[k]
        return remote(
            self.total.at[self.cells(part, source)],
            lands.at[(part, *place)],
            self.send.at[part, k],
            self.recv.at[part, k],
            self.torus.device(ORDERS[part][slot], delta),
        )

    def start(self, part, *ks):
        for k in ks:
            copy = self.copy(part, k)
            copy.start()
            self.started.append(copy)

    def landed(self, part, k):
        self.copy(part, k).wait_recv()
        _, _, _, lands, place = self.specs[k]
        return lands[(part, *place)].astype(F32)

    def add(self, part, offsets, ks):
        idx = self.cells(part, offsets)
        value = self.total[idx].astype(F32)
        for k in ks:
            value = value + self.landed(part, k)
        return idx, value

    def run(self, produce, finish):
        parts = range(PARTS)
        plane = {d: 3 * i for i, d in enumerate(INWARD)}

        def raw(p, way):
            for d in INWARD:
                if FAR_WAY[d] != way:
                    self.start(p, plane[d] + (1 if way == 1 else 2))

        for p in parts:
            produce(p, 2)
            self.start(p, *(plane[d] for d in INWARD))
        for p in parts:
            produce(p, 1)
            raw(p, 1)
            produce(p, -1)
            raw(p, -1)
        for d in INWARD:
            way = FAR_WAY[d]
            for p in parts:
                idx, value = self.add(p, (None, d, way), (plane[d],))
                self.total[idx] = value.astype(BF16)
                self.start(p, plane[d] + (1 if way == 1 else 2))
        for p in parts:
            produce(p, 0)
        for i, d in enumerate(INWARD):
            for p in parts:
                idx, value = self.add(p, (None, d, 0), (plane[d] + 1, plane[d] + 2))
                self.total[idx] = value.astype(BF16)
                if d:
                    self.start(p, 12 + i)
        for p in parts:
            idx, value = self.add(p, (None, 0, 0), (12, 13, 14))
            self.total[idx] = value.astype(BF16)
            self.start(p, 15, 16, 17)
        for p in parts:
            _, value = self.add(p, (0, 0, 0), (15, 16, 17))
            finish(p, value)

    def drain(self):
        for copy in self.started:
            copy.wait_send()


MOVES = (
    (2, 2), (1, 2), (3, 2), (2, 1), (2, 3), (0, 2), (2, 0), (1, 1),
    (1, 3), (3, 1), (3, 3), (0, 1), (0, 3), (1, 0), (3, 0), (0, 0),
)
HALF = len(MOVES) // 2
TILE = 768
HIDDEN_TILE = 512
SPLIT = (0, 896, 1664, 2304)


def tiles(size, body, tile=TILE):
    def step(i, carry):
        body(pl.ds(pl.multiple_of(i * tile, tile), tile))
        return carry

    lax.fori_loop(0, size // tile, step, 0)


def layer_kernel(
    tokens_hbm, ids_hbm, weights_hbm, gate_hbm, up_hbm, down_hbm, sgate_hbm, sup_hbm, sdown_hbm,
    enc_hbm, bias_hbm, dec_hbm, feat_hbm, rec_ref,
    gate, up, down, sgate, sup, sdown, meta, metas, partial, combine, outgoing, received, hidden, served, returned,
    parts_out, parts_in, gathered0, gathered1, gathered2, total, planes, lines, blocks, scores, feats, enc, dec, bias,
    tokens_ref, ids_ref, weights_ref, local_sem, meta_send, meta_recv, go_send, go_recv, back_send, back_recv, part_send, part_recv,
    ag_send, ag_recv, rs_send, rs_recv, cross_send, cross_recv,
):
    torus = Torus()
    e, f, core, other, partner = torus.e, torus.f, torus.core, torus.other, torus.partner
    n_e, own_rows, model = outgoing.shape
    n_f = metas.shape[0]
    rows = n_f * own_rows
    slots = n_e * own_rows
    chunk = HALF * own_rows
    width = total.shape[-1]
    gathered = (gathered0, gathered1, gathered2)
    features = enc.shape[2]

    weight_copies = [
        pltpu.make_async_copy(src, dst, local_sem.at[i])
        for i, (src, dst) in enumerate(
            (
                (sgate_hbm, sgate), (sup_hbm, sup), (sdown_hbm, sdown),
                (gate_hbm.at[0], gate), (up_hbm.at[0], up), (down_hbm.at[0], down),
                (enc_hbm, enc.at[core]), (bias_hbm, bias.at[core]), (dec_hbm, dec.at[core]),
            )
        )
    ]
    tokens_copy = pltpu.make_async_copy(tokens_hbm, tokens_ref, local_sem.at[10])
    feat_sem = local_sem.at[9]

    choice_copies = [
        pltpu.make_async_copy(ids_hbm, ids_ref, local_sem.at[11]),
        pltpu.make_async_copy(weights_hbm, weights_ref, local_sem.at[12]),
    ]
    for copy in choice_copies + [tokens_copy] + weight_copies:
        copy.start()

    def plane(move, sign=1):
        dy, dx = move
        y = lax.rem(torus.pos[0] + SIDE + sign * dy, SIDE)
        return y * SIDE + lax.rem(torus.pos[1] + SIDE + sign * dx, SIDE)

    def column(i):
        return lax.rem(f + i, n_f)

    barrier = pltpu.get_barrier_semaphore()
    peers = [(plane(m), f) for m in MOVES[:-1]] + [(e, column(i)) for i in range(1, n_f)]
    for there in peers:
        pl.semaphore_signal(barrier, inc=1, device_id=there, device_id_type=MESH)
    for copy in choice_copies:
        copy.wait()
    meta[...] = jnp.zeros_like(meta)
    meta[:TOP, :own_rows] = ids_ref[...].astype(F32)
    meta[TOP:, :own_rows] = weights_ref[...]
    metas[f] = meta[...]
    pl.semaphore_wait(barrier, len(peers))
    sent = []

    def send(copy):
        copy.start()
        sent.append(copy)

    for i in range(1, n_f):
        send(remote(meta, metas.at[f], meta_send.at[i - 1], meta_recv.at[i - 1], (e, column(i))))

    for copy in weight_copies[:3]:
        copy.wait()
    tokens_copy.wait()
    tokens = tokens_ref[...]
    shared_gate = jnp.dot(tokens, sgate[...], preferred_element_type=F32)
    shared_up = jnp.dot(tokens, sup[...], preferred_element_type=F32)
    shared_hidden = (jax.nn.silu(shared_gate) * shared_up).astype(BF16)

    for i in range(1, n_f):
        src = column(n_f - i)
        remote(metas.at[src], metas.at[src], meta_send.at[i - 1], meta_recv.at[i - 1], (e, src)).wait_recv()
    turned = metas[...].reshape(rows, metas.shape[2]).T[:own_rows]
    table = jnp.concatenate(
        [turned] + [pltpu.roll(turned, rows - own_rows * i, 1) for i in range(1, n_f)], axis=0
    )
    slot = lax.broadcasted_iota(jnp.int32, (rows, slots), 1)
    token = lax.broadcasted_iota(jnp.int32, (rows, slots), 0)
    column_slot = lax.broadcasted_iota(jnp.int32, (1, slots), 1) // own_rows
    wanted = jnp.zeros((1, slots), jnp.int32)
    for i, move in enumerate(MOVES):
        wanted = jnp.where(column_slot == i, plane(move) * n_f + f, wanted)
    wanted = wanted.astype(F32)
    named = jnp.zeros((rows, slots), F32)
    weight = jnp.zeros((rows, slots), F32)
    for k in range(TOP):
        same = table[:, k : k + 1] == wanted
        named = named + jnp.where(same, 1.0, 0.0)
        weight = weight + jnp.where(same, table[:, TOP + k : TOP + k + 1], 0.0)
    row = lax.broadcasted_iota(jnp.int32, (rows, rows), 0)
    col = lax.broadcasted_iota(jnp.int32, (rows, rows), 1)
    before = jnp.where((row // own_rows == col // own_rows) & (col < row), 1.0, 0.0).astype(BF16)
    rank = jnp.dot(before, named.astype(BF16), preferred_element_type=F32)
    here = (lax.rem(slot, 2).astype(F32) == rank) & (lax.rem(slot // 2, n_f) == token // own_rows)
    places = jnp.where(here, named, 0.0)
    weight = places * weight
    high = weight.astype(BF16)
    combine[0] = high
    combine[1] = (weight - high.astype(F32)).astype(BF16)
    dispatch = places.T.astype(BF16)

    halves = (range(HALF), range(HALF, n_e - 1))

    def span(half):
        return slice(half * HALF, (half + 1) * HALF)

    for half in range(2):
        mine = dispatch[half * chunk : (half + 1) * chunk]

        def pick(cols, half=half, mine=mine):
            value = jnp.dot(mine, tokens_ref[:, cols], preferred_element_type=F32)
            value = value.astype(BF16).reshape(HALF, own_rows, TILE)
            outgoing[span(half), :, cols] = value
            if half:
                received[n_e - 1, :, cols] = value[HALF - 1]

        tiles(model, pick)
        for i in halves[half]:
            send(remote(outgoing.at[i], received.at[i], go_send.at[i], go_recv.at[i], (plane(MOVES[i]), f)))

    for copy in weight_copies[6:]:
        copy.wait()
    cross_copies = [
        remote(ref.at[core], ref.at[core], cross_send.at[i], cross_recv.at[i], partner)
        for i, ref in enumerate((enc, bias, dec))
    ]
    for copy in cross_copies:
        send(copy)

    def shared(cols):
        value = jnp.dot(shared_hidden, sdown[:, cols], preferred_element_type=F32)
        partial[:, :, cols] = value.reshape(n_f, own_rows, TILE)

    tiles(model, shared)
    for copy in weight_copies[3:6]:
        copy.wait()

    for half in range(2):
        for i in halves[half]:
            remote(
                outgoing.at[i], received.at[i], go_send.at[i], go_recv.at[i], (plane(MOVES[i], -1), f)
            ).wait_recv()

        def inner(cols, half=half):
            x = received[span(half)].reshape(chunk, model)
            gate_proj = jnp.dot(x, gate[:, cols], preferred_element_type=F32)
            up_proj = jnp.dot(x, up[:, cols], preferred_element_type=F32)
            hidden[half, :, cols] = (jax.nn.silu(gate_proj) * up_proj).astype(BF16)

        tiles(hidden.shape[2], inner, HIDDEN_TILE)

    def part_cols(p):
        return pl.ds(SPLIT[p], SPLIT[p + 1] - SPLIT[p])

    def back_copy(p, i, sign):
        cols = part_cols(p)
        return remote(
            served.at[i, :, cols], returned.at[i, :, cols],
            back_send.at[p, i], back_recv.at[p, i], (plane(MOVES[i], sign), f),
        )

    def outer(cols):
        value = jnp.dot(hidden[...].reshape(slots, hidden.shape[2]), down[:, cols], preferred_element_type=F32)
        value = value.astype(BF16).reshape(n_e, own_rows, -1)
        served[:, :, cols] = value
        returned[n_e - 1, :, cols] = value[n_e - 1]

    for p in range(PARTS):
        outer(part_cols(p))
        for i in range(n_e - 1):
            send(back_copy(p, i, -1))

    def fill(y, carry):
        for which in range(2):
            scores[which, y] = jnp.broadcast_to(bias[which], (SIDE, SIDE, own_rows, features))
        return carry

    for copy in cross_copies:
        copy.wait_recv()
    lax.fori_loop(0, SIDE, fill, 0)

    gather = Gather(torus, gathered, ag_send, ag_recv)
    incoming = {}

    def share(cols):
        back = returned[:, :, cols].reshape(slots, -1)
        value = partial[:, :, cols].reshape(rows, -1)
        for i in range(2):
            value = value + jnp.dot(combine[i], back, preferred_element_type=F32)
        value = value.reshape(n_f, own_rows, -1)
        partial[:, :, cols] = value
        parts_out[:, :, cols] = value.astype(BF16)

    def give(p):
        for i in range(n_e - 1):
            back_copy(p, i, 1).wait_recv()
        cols = part_cols(p)
        share(cols)
        for i in range(1, n_f):
            there = column(i)
            copy = remote(
                parts_out.at[there, :, cols], parts_in.at[i - 1, :, cols],
                part_send.at[p, i - 1], part_recv.at[p, i - 1], (e, there),
            )
            send(copy)
            incoming[p, i] = copy

    def take(p):
        cols = part_cols(p)
        value = partial[f, :, cols]
        for i in range(1, n_f):
            incoming[p, i].wait_recv()
            value = value + parts_in[i - 1, :, cols].astype(F32)
        gathered[p][torus.pos] = value.astype(BF16)
        gather.start(p, 0, 1, 2)

    def encode(p, delta):
        idx = torus.index(p, (None, None, delta))

        block = gathered[p][idx].reshape(SIDE * SIDE * own_rows, -1)
        for which in range(2):
            value = jnp.dot(block, enc[which, SPLIT[p] : SPLIT[p + 1], :], preferred_element_type=F32)
            at = (which, *idx)
            scores[at] = scores[at] + value.reshape(SIDE, SIDE, own_rows, features)

    steps = [gather.steps(p) for p in range(PARTS)]
    early = [
        [functools.partial(give, p), functools.partial(take, p), *steps[p][:3]] for p in range(PARTS)
    ]
    for turn in range(len(early[0]) + PARTS - 1):
        for p in reversed(range(PARTS)):
            if 0 <= turn - p < len(early[p]):
                early[p][turn - p]()
    for p in range(PARTS):
        encode(p, 0)
    for i in range(3):
        for p in range(PARTS):
            steps[p][3][i]()
    for p in range(PARTS):
        encode(p, -1)
        encode(p, 1)
    for p in range(PARTS):
        steps[p][4]()
        encode(p, 2)

    def rectify(delta):
        idx = torus.index(0, (None, None, delta))
        for which in range(2):
            feats[(which, *idx)] = jnp.maximum(scores[(which, *idx)], 0.0).astype(BF16)

    own_out = pltpu.make_async_copy(feats.at[core], feat_hbm.at[:, :, :, core], feat_sem)
    cross_out = remote(
        feats.at[other], feat_hbm.at[:, :, :, core], cross_send.at[3], cross_recv.at[3], partner
    )
    cross_in = remote(
        feats.at[other], feat_hbm.at[:, :, :, other], cross_send.at[3], cross_recv.at[3], partner
    )

    scatter = Scatter(torus, total, planes, lines, blocks, rs_send, rs_recv)

    def produce(p, delta):
        if (p, delta) == (0, 2):
            rectify(2)
        if (p, delta) == (1, 2):
            for d in (0, 1, -1):
                rectify(d)
            own_out.start()
            cross_out.start()
        idx = torus.index(p, (None, None, delta))
        value = 0.0
        for which in range(2):
            block = feats[(which, *idx)].reshape(SIDE * SIDE * own_rows, features)
            value = value + jnp.dot(
                block, dec[which, :, p * width : (p + 1) * width], preferred_element_type=F32
            )
        total[(p, *idx)] = value.astype(BF16).reshape(SIDE, SIDE, own_rows, width)

    def finish(p, value):
        rec_ref[:, p * width : (p + 1) * width] = value

    scatter.run(produce, finish)

    own_out.wait()
    cross_out.wait_send()
    cross_in.wait_recv()
    for copy in sent:
        copy.wait_send()
    gather.drain()
    scatter.drain()


def layer(tokens, ids, weights, routed, shared, encoder, encoder_bias, decoder):
    n_e, n_f = lax.axis_size("expert"), lax.axis_size("feat")
    own_rows = ids.shape[1]
    model = tokens.shape[1]
    hid = routed[0].shape[2]
    slots = n_e * own_rows
    rows = n_f * own_rows
    features = encoder.shape[1]
    width = model // PARTS
    cube = (SIDE, SIDE, SIDE)
    vmem = pl.BlockSpec(memory_space=pltpu.VMEM)
    hbm = pl.BlockSpec(memory_space=pl.ANY)
    dma = pltpu.SemaphoreType.DMA
    plane_rows = pltpu.VMEM((n_e, own_rows, model), BF16)
    torus_sem = dma((PARTS, COPIES))
    return pl.pallas_call(
        layer_kernel,
        name="layer",
        out_shape=(
            jax.ShapeDtypeStruct((*cube, 2, own_rows, features), BF16),
            jax.ShapeDtypeStruct((own_rows, model), F32),
        ),
        in_specs=[hbm] * 12,
        out_specs=(hbm, vmem),
        scratch_shapes=[pltpu.VMEM(w.shape[1:], BF16) for w in routed]
        + [pltpu.VMEM(w.shape, BF16) for w in shared]
        + [
            pltpu.VMEM((2 * TOP, rows), F32),
            pltpu.VMEM((n_f, 2 * TOP, rows), F32),
            pltpu.VMEM((n_f, own_rows, model), F32),
            pltpu.VMEM((2, rows, slots), BF16),
            plane_rows,
            plane_rows,
            pltpu.VMEM((2, HALF * own_rows, hid), BF16),
            plane_rows,
            plane_rows,
            pltpu.VMEM((n_f, own_rows, model), BF16),
            pltpu.VMEM((n_f - 1, own_rows, model), BF16),
            *(pltpu.VMEM((*cube, own_rows, SPLIT[p + 1] - SPLIT[p]), BF16) for p in range(PARTS)),
            pltpu.VMEM((PARTS, *cube, own_rows, width), BF16),
            pltpu.VMEM((PARTS, 3, SIDE, SIDE, own_rows, width), BF16),
            pltpu.VMEM((PARTS, 3, SIDE, own_rows, width), BF16),
            pltpu.VMEM((PARTS, 3, own_rows, width), BF16),
            pltpu.VMEM((2, *cube, own_rows, features), F32),
            pltpu.VMEM((2, *cube, own_rows, features), BF16),
            pltpu.VMEM((2, model, features), BF16),
            pltpu.VMEM((2, features, model), BF16),
            pltpu.VMEM((2, 1, features), F32),
            pltpu.VMEM(tokens.shape, BF16),
            pltpu.VMEM(ids.shape, ids.dtype),
            pltpu.VMEM(weights.shape, weights.dtype),
            dma((13,)),
            dma((n_f - 1,)),
            dma((n_f - 1,)),
            dma((n_e - 1,)),
            dma((n_e - 1,)),
            dma((PARTS, n_e - 1)),
            dma((PARTS, n_e - 1)),
            dma((PARTS, n_f - 1)),
            dma((PARTS, n_f - 1)),
            torus_sem, torus_sem, torus_sem, torus_sem,
            dma((4,)),
            dma((4,)),
        ],
        compiler_params=pltpu.CompilerParams(
            collective_id=0, has_side_effects=True, vmem_limit_bytes=63 * 1024 * 1024
        ),
    )(tokens, ids, weights, *routed, *shared, encoder, encoder_bias, decoder)


def finish_kernel(feat_hbm, sums_hbm, bias_hbm, out_hbm, rec_hbm, held, sums, bias, in_sem, out_sem):
    reads = [
        pltpu.make_async_copy(sums_hbm, sums, in_sem.at[SIDE]),
        pltpu.make_async_copy(bias_hbm, bias, in_sem.at[SIDE + 1]),
    ] + [pltpu.make_async_copy(feat_hbm.at[y], held.at[y], in_sem.at[y]) for y in range(SIDE)]
    writes = [pltpu.make_async_copy(sums, rec_hbm, out_sem.at[SIDE])] + [
        pltpu.make_async_copy(held.at[y], out_hbm.at[y], out_sem.at[y]) for y in range(SIDE)
    ]
    for copy in reads:
        copy.start()
    reads[0].wait()
    reads[1].wait()
    lanes = bias.shape[1]
    for i in range(bias.shape[0]):
        cols = slice(i * lanes, (i + 1) * lanes)
        sums[:, cols] = sums[:, cols] + bias[i : i + 1, :]
    for y in range(SIDE):
        reads[2 + y].wait()
        writes[1 + y].start()
    writes[0].start()
    for copy in writes:
        copy.wait()


def finish(features, sums, bias):
    hbm = pl.BlockSpec(memory_space=pl.ANY)
    bias = bias.reshape(-1, 128)
    return pl.pallas_call(
        finish_kernel,
        name="finish",
        out_shape=(
            jax.ShapeDtypeStruct(features.shape, features.dtype),
            jax.ShapeDtypeStruct(sums.shape, sums.dtype),
        ),
        in_specs=[hbm] * 3,
        out_specs=(hbm, hbm),
        scratch_shapes=[
            pltpu.VMEM(features.shape, features.dtype),
            pltpu.VMEM(sums.shape, sums.dtype),
            pltpu.VMEM(bias.shape, bias.dtype),
            pltpu.SemaphoreType.DMA((SIDE + 2,)),
            pltpu.SemaphoreType.DMA((SIDE + 1,)),
        ],
        compiler_params=pltpu.CompilerParams(vmem_limit_bytes=60 * 1024 * 1024),
    )(features, sums, bias)


def shards(
    tokens,
    expert_ids,
    gate_weights,
    expert_gate,
    expert_up,
    expert_down,
    shared_gate,
    shared_up,
    shared_down,
    encoder,
    encoder_bias,
    decoder,
    decoder_bias,
):
    features, sums = layer(
        tokens,
        expert_ids.T,
        gate_weights.T,
        (expert_gate, expert_up, expert_down),
        (shared_gate, shared_up, shared_down),
        encoder,
        encoder_bias[None, :],
        decoder,
    )
    features, sums = finish(features, sums, decoder_bias)
    return features.reshape(-1, encoder.shape[1]), sums


def solution(mesh):
    return jax.shard_map(
        shards,
        mesh=mesh,
        in_specs=(
            P("expert", None),
            P(("expert", "feat"), None),
            P(("expert", "feat"), None),
            P(("expert", "feat"), None, None),
            P(("expert", "feat"), None, None),
            P(("expert", "feat"), None, None),
            P(None, "feat"),
            P(None, "feat"),
            P("feat", None),
            P(None, ("expert", "feat")),
            P(("expert", "feat")),
            P(("expert", "feat"), None),
            P(),
        ),
        out_specs=(P(None, ("expert", "feat")), P(("expert", "feat"), None)),
        check_vma=False,
    )
```

```python
import functools

import jax
import jax.numpy as jnp
from jax import lax
from jax.experimental import pallas as pl
from jax.experimental.pallas import tpu as pltpu
from jax.sharding import PartitionSpec as P

MESH = pl.DeviceIdType.MESH
SIDE = 4
ORDERS = ((1, 0, 2), (0, 2, 1), (2, 1, 0))
PARTS = len(ORDERS)
ALL = slice(None)
BF16 = jnp.bfloat16
F32 = jnp.float32
OUTWARD = (0, 1, -1, 2)
INWARD = (2, 1, -1, 0)
FAR_WAY = {0: 1, 2: 1, 1: -1, -1: -1}
FAR, MINUS, PLUS = 0, 1, 2
OTHERS = (1, -1, 2)
TOP = 8
COPIES = 18


class Torus:
    def __init__(self):
        self.e, self.f = lax.axis_index("expert"), lax.axis_index("feat")
        self.core = lax.rem(self.f, 2)
        self.other = 1 - self.core
        self.pos = (self.e // SIDE, lax.rem(self.e, SIDE), self.f // 2)
        self.partner = (self.e, self.f + 1 - 2 * self.core)

    def at(self, axis, delta):
        return lax.rem(self.pos[axis] + delta + SIDE, SIDE) if delta else self.pos[axis]

    def device(self, axis, delta):
        there = list(self.pos)
        there[axis] = self.at(axis, delta)
        return (there[0] * SIDE + there[1], there[2] * 2 + self.core)

    def index(self, part, offsets):
        idx = [None] * 3
        for axis, delta in zip(ORDERS[part], offsets):
            idx[axis] = ALL if delta is None else self.at(axis, delta)
        return tuple(idx)


def remote(src, dst, send, recv, where):
    return pltpu.make_async_remote_copy(
        src_ref=src, dst_ref=dst, send_sem=send, recv_sem=recv, device_id=where, device_id_type=MESH
    )


class Gather:
    def __init__(self, torus, bufs, send, recv):
        self.torus, self.bufs, self.send, self.recv = torus, bufs, send, recv
        self.specs = [(0, d, (0, 0, 0), (-d, 0, 0)) for d in OTHERS]
        self.specs += [(1, d, (None, 0, 0), (None, -d, 0)) for d in OTHERS]
        for d in OUTWARD:
            way = FAR_WAY[d]
            self.specs += [
                (2, 1, (None, d, 0), (None, d, -1)),
                (2, -1, (None, d, 0), (None, d, 1)),
                (2, way, (None, d, -way), (None, d, 2)),
            ]
        self.started = []

    def cells(self, part, offsets):
        return self.bufs[part].at[self.torus.index(part, offsets)]

    def copy(self, part, k, landing):
        slot, delta, source, target = self.specs[k]
        cells = self.cells(part, target if landing else source)
        return remote(
            cells, cells, self.send.at[part, k], self.recv.at[part, k], self.torus.device(ORDERS[part][slot], delta)
        )

    def start(self, part, *ks):
        for k in ks:
            copy = self.copy(part, k, False)
            copy.start()
            self.started.append(copy)

    def wait(self, part, *ks):
        for k in ks:
            self.copy(part, k, True).wait_recv()

    def steps(self, p):
        plane = {d: 6 + 3 * i for i, d in enumerate(OUTWARD)}

        def go_on(d):
            self.wait(p, plane[d], plane[d] + 1)
            self.start(p, plane[d] + 2)

        def lines():
            self.wait(p, 0, 1, 2)
            self.start(p, 3, 4, 5, plane[0], plane[0] + 1)

        def near_planes():
            for k, d in ((3, -1), (4, 1)):
                self.wait(p, k)
                self.start(p, plane[d], plane[d] + 1)
            go_on(0)

        def far_planes():
            self.wait(p, 5)
            self.start(p, plane[2], plane[2] + 1)

        def far_arrivals():
            self.wait(p, *(plane[d] + 2 for d in OUTWARD))

        return lines, near_planes, far_planes, [functools.partial(go_on, d) for d in (-1, 1, 2)], far_arrivals

    def drain(self):
        for copy in self.started:
            copy.wait_send()


class Scatter:
    def __init__(self, torus, total, planes, lines, blocks, send, recv):
        self.torus, self.total, self.send, self.recv = torus, total, send, recv
        self.specs = []
        for i, d in enumerate(INWARD):
            for way, last, kind in ((FAR_WAY[d], 2, FAR), (1, 1, MINUS), (-1, -1, PLUS)):
                self.specs.append((2, way, (None, d, last), planes, (kind, i)))
        self.specs += [(1, d, (None, d, 0), lines, (i,)) for i, d in enumerate(INWARD[:3])]
        self.specs += [(0, d, (d, 0, 0), blocks, (i,)) for i, d in enumerate(INWARD[:3])]
        self.started = []

    def cells(self, part, offsets):
        return (part, *self.torus.index(part, offsets))

    def copy(self, part, k):
        slot, delta, source, lands, place = self.specs[k]
        return remote(
            self.total.at[self.cells(part, source)],
            lands.at[(part, *place)],
            self.send.at[part, k],
            self.recv.at[part, k],
            self.torus.device(ORDERS[part][slot], delta),
        )

    def start(self, part, *ks):
        for k in ks:
            copy = self.copy(part, k)
            copy.start()
            self.started.append(copy)

    def landed(self, part, k):
        self.copy(part, k).wait_recv()
        _, _, _, lands, place = self.specs[k]
        return lands[(part, *place)].astype(F32)

    def add(self, part, offsets, ks):
        idx = self.cells(part, offsets)
        value = self.total[idx].astype(F32)
        for k in ks:
            value = value + self.landed(part, k)
        return idx, value

    def run(self, produce, finish):
        parts = range(PARTS)
        plane = {d: 3 * i for i, d in enumerate(INWARD)}

        def raw(p, way):
            for d in INWARD:
                if FAR_WAY[d] != way:
                    self.start(p, plane[d] + (1 if way == 1 else 2))

        for p in parts:
            produce(p, 2)
            self.start(p, *(plane[d] for d in INWARD))
        for p in parts:
            produce(p, 1)
            raw(p, 1)
            produce(p, -1)
            raw(p, -1)
        for d in INWARD:
            way = FAR_WAY[d]
            for p in parts:
                idx, value = self.add(p, (None, d, way), (plane[d],))
                self.total[idx] = value.astype(BF16)
                self.start(p, plane[d] + (1 if way == 1 else 2))
        for p in parts:
            produce(p, 0)
        for i, d in enumerate(INWARD):
            for p in parts:
                idx, value = self.add(p, (None, d, 0), (plane[d] + 1, plane[d] + 2))
                self.total[idx] = value.astype(BF16)
                if d:
                    self.start(p, 12 + i)
        for p in parts:
            idx, value = self.add(p, (None, 0, 0), (12, 13, 14))
            self.total[idx] = value.astype(BF16)
            self.start(p, 15, 16, 17)
        for p in parts:
            _, value = self.add(p, (0, 0, 0), (15, 16, 17))
            finish(p, value)

    def drain(self):
        for copy in self.started:
            copy.wait_send()


MOVES = (
    (2, 2), (1, 2), (3, 2), (2, 1), (2, 3), (0, 2), (2, 0), (1, 1),
    (1, 3), (3, 1), (3, 3), (0, 1), (0, 3), (1, 0), (3, 0), (0, 0),
)
HALF = len(MOVES) // 2
TILE = 768
HIDDEN_TILE = 512
SPLIT = (0, 1024, 1792, 2304)


def tiles(size, body, tile=TILE):
    def step(i, carry):
        body(pl.ds(pl.multiple_of(i * tile, tile), tile))
        return carry

    lax.fori_loop(0, size // tile, step, 0)


def layer_kernel(
    tokens_hbm, ids_hbm, weights_hbm, gate_hbm, up_hbm, down_hbm, sgate_hbm, sup_hbm, sdown_hbm,
    enc_hbm, bias_hbm, dec_hbm, feat_hbm, rec_ref,
    gate, up, down, sgate, sup, sdown, meta, metas, partial, combine, outgoing, received, hidden, served, returned,
    parts_out, parts_in, gathered0, gathered1, gathered2, total, planes, lines, blocks, scores, feats, enc, dec, bias,
    tokens_ref, ids_ref, weights_ref, local_sem, meta_send, meta_recv, go_send, go_recv, back_send, back_recv, part_send, part_recv,
    ag_send, ag_recv, rs_send, rs_recv, cross_send, cross_recv,
):
    torus = Torus()
    e, f, core, other, partner = torus.e, torus.f, torus.core, torus.other, torus.partner
    n_e, own_rows, model = outgoing.shape
    n_f = metas.shape[0]
    rows = n_f * own_rows
    slots = n_e * own_rows
    chunk = HALF * own_rows
    width = total.shape[-1]
    gathered = (gathered0, gathered1, gathered2)
    features = enc.shape[2]

    weight_copies = [
        pltpu.make_async_copy(src, dst, local_sem.at[i])
        for i, (src, dst) in enumerate(
            (
                (sgate_hbm, sgate), (sup_hbm, sup), (sdown_hbm, sdown),
                (gate_hbm.at[0], gate), (up_hbm.at[0], up), (down_hbm.at[0], down),
                (enc_hbm, enc.at[core]), (bias_hbm, bias.at[core]), (dec_hbm, dec.at[core]),
            )
        )
    ]
    tokens_copy = pltpu.make_async_copy(tokens_hbm, tokens_ref, local_sem.at[10])
    feat_sem = local_sem.at[9]

    choice_copies = [
        pltpu.make_async_copy(ids_hbm, ids_ref, local_sem.at[11]),
        pltpu.make_async_copy(weights_hbm, weights_ref, local_sem.at[12]),
    ]
    for copy in choice_copies + [tokens_copy] + weight_copies:
        copy.start()

    def plane(move, sign=1):
        dy, dx = move
        y = lax.rem(torus.pos[0] + SIDE + sign * dy, SIDE)
        return y * SIDE + lax.rem(torus.pos[1] + SIDE + sign * dx, SIDE)

    def column(i):
        return lax.rem(f + i, n_f)

    barrier = pltpu.get_barrier_semaphore()
    peers = [(plane(m), f) for m in MOVES[:-1]] + [(e, column(i)) for i in range(1, n_f)]
    for there in peers:
        pl.semaphore_signal(barrier, inc=1, device_id=there, device_id_type=MESH)
    for copy in choice_copies:
        copy.wait()
    meta[...] = jnp.zeros_like(meta)
    meta[:TOP, :own_rows] = ids_ref[...].astype(F32)
    meta[TOP:, :own_rows] = weights_ref[...]
    metas[f] = meta[...]
    pl.semaphore_wait(barrier, len(peers))
    sent = []

    def send(copy):
        copy.start()
        sent.append(copy)

    for i in range(1, n_f):
        send(remote(meta, metas.at[f], meta_send.at[i - 1], meta_recv.at[i - 1], (e, column(i))))

    for copy in weight_copies[:3]:
        copy.wait()
    tokens_copy.wait()
    tokens = tokens_ref[...]
    shared_gate = jnp.dot(tokens, sgate[...], preferred_element_type=F32)
    shared_up = jnp.dot(tokens, sup[...], preferred_element_type=F32)
    shared_hidden = (jax.nn.silu(shared_gate) * shared_up).astype(BF16)

    for i in range(1, n_f):
        src = column(n_f - i)
        remote(metas.at[src], metas.at[src], meta_send.at[i - 1], meta_recv.at[i - 1], (e, src)).wait_recv()
    turned = metas[...].reshape(rows, metas.shape[2]).T[:own_rows]
    table = jnp.concatenate(
        [turned] + [pltpu.roll(turned, rows - own_rows * i, 1) for i in range(1, n_f)], axis=0
    )
    slot = lax.broadcasted_iota(jnp.int32, (rows, slots), 1)
    token = lax.broadcasted_iota(jnp.int32, (rows, slots), 0)
    column_slot = lax.broadcasted_iota(jnp.int32, (1, slots), 1) // own_rows
    wanted = jnp.zeros((1, slots), jnp.int32)
    for i, move in enumerate(MOVES):
        wanted = jnp.where(column_slot == i, plane(move) * n_f + f, wanted)
    wanted = wanted.astype(F32)
    named = jnp.zeros((rows, slots), F32)
    weight = jnp.zeros((rows, slots), F32)
    for k in range(TOP):
        same = table[:, k : k + 1] == wanted
        named = named + jnp.where(same, 1.0, 0.0)
        weight = weight + jnp.where(same, table[:, TOP + k : TOP + k + 1], 0.0)
    row = lax.broadcasted_iota(jnp.int32, (rows, rows), 0)
    col = lax.broadcasted_iota(jnp.int32, (rows, rows), 1)
    before = jnp.where((row // own_rows == col // own_rows) & (col < row), 1.0, 0.0).astype(BF16)
    rank = jnp.dot(before, named.astype(BF16), preferred_element_type=F32)
    here = (lax.rem(slot, 2).astype(F32) == rank) & (lax.rem(slot // 2, n_f) == token // own_rows)
    places = jnp.where(here, named, 0.0)
    weight = places * weight
    high = weight.astype(BF16)
    combine[0] = high
    combine[1] = (weight - high.astype(F32)).astype(BF16)
    dispatch = places.T.astype(BF16)

    halves = (range(HALF), range(HALF, n_e - 1))

    def span(half):
        return slice(half * HALF, (half + 1) * HALF)

    for half in range(2):
        mine = dispatch[half * chunk : (half + 1) * chunk]

        def pick(cols, half=half, mine=mine):
            value = jnp.dot(mine, tokens_ref[:, cols], preferred_element_type=F32)
            value = value.astype(BF16).reshape(HALF, own_rows, TILE)
            outgoing[span(half), :, cols] = value
            if half:
                received[n_e - 1, :, cols] = value[HALF - 1]

        tiles(model, pick)
        for i in halves[half]:
            send(remote(outgoing.at[i], received.at[i], go_send.at[i], go_recv.at[i], (plane(MOVES[i]), f)))

    for copy in weight_copies[6:]:
        copy.wait()
    cross_copies = [
        remote(ref.at[core], ref.at[core], cross_send.at[i], cross_recv.at[i], partner)
        for i, ref in enumerate((enc, bias, dec))
    ]
    for copy in cross_copies:
        send(copy)

    def shared(cols):
        value = jnp.dot(shared_hidden, sdown[:, cols], preferred_element_type=F32)
        partial[:, :, cols] = value.reshape(n_f, own_rows, TILE)

    tiles(model, shared)
    for copy in weight_copies[3:6]:
        copy.wait()

    for half in range(2):
        for i in halves[half]:
            remote(
                outgoing.at[i], received.at[i], go_send.at[i], go_recv.at[i], (plane(MOVES[i], -1), f)
            ).wait_recv()

        def inner(cols, half=half):
            x = received[span(half)].reshape(chunk, model)
            gate_proj = jnp.dot(x, gate[:, cols], preferred_element_type=F32)
            up_proj = jnp.dot(x, up[:, cols], preferred_element_type=F32)
            hidden[half, :, cols] = (jax.nn.silu(gate_proj) * up_proj).astype(BF16)

        tiles(hidden.shape[2], inner, HIDDEN_TILE)

    def part_cols(p):
        return pl.ds(SPLIT[p], SPLIT[p + 1] - SPLIT[p])

    def back_copy(p, i, sign):
        cols = part_cols(p)
        return remote(
            served.at[i, :, cols], returned.at[i, :, cols],
            back_send.at[p, i], back_recv.at[p, i], (plane(MOVES[i], sign), f),
        )

    def outer(cols):
        value = jnp.dot(hidden[...].reshape(slots, hidden.shape[2]), down[:, cols], preferred_element_type=F32)
        value = value.astype(BF16).reshape(n_e, own_rows, -1)
        served[:, :, cols] = value
        returned[n_e - 1, :, cols] = value[n_e - 1]

    for p in range(PARTS):
        outer(part_cols(p))
        for i in range(n_e - 1):
            send(back_copy(p, i, -1))

    def fill(y, carry):
        for which in range(2):
            scores[which, y] = jnp.broadcast_to(bias[which], (SIDE, SIDE, own_rows, features))
        return carry

    for copy in cross_copies:
        copy.wait_recv()
    lax.fori_loop(0, SIDE, fill, 0)

    gather = Gather(torus, gathered, ag_send, ag_recv)
    incoming = {}

    def share(cols):
        back = returned[:, :, cols].reshape(slots, -1)
        value = partial[:, :, cols].reshape(rows, -1)
        for i in range(2):
            value = value + jnp.dot(combine[i], back, preferred_element_type=F32)
        value = value.reshape(n_f, own_rows, -1)
        partial[:, :, cols] = value
        parts_out[:, :, cols] = value.astype(BF16)

    def give(p):
        for i in range(n_e - 1):
            back_copy(p, i, 1).wait_recv()
        cols = part_cols(p)
        share(cols)
        for i in range(1, n_f):
            there = column(i)
            copy = remote(
                parts_out.at[there, :, cols], parts_in.at[i - 1, :, cols],
                part_send.at[p, i - 1], part_recv.at[p, i - 1], (e, there),
            )
            send(copy)
            incoming[p, i] = copy

    def take(p):
        cols = part_cols(p)
        value = partial[f, :, cols]
        for i in range(1, n_f):
            incoming[p, i].wait_recv()
            value = value + parts_in[i - 1, :, cols].astype(F32)
        gathered[p][torus.pos] = value.astype(BF16)
        gather.start(p, 0, 1, 2)

    def encode(p, delta):
        idx = torus.index(p, (None, None, delta))

        block = gathered[p][idx].reshape(SIDE * SIDE * own_rows, -1)
        for which in range(2):
            value = jnp.dot(block, enc[which, SPLIT[p] : SPLIT[p + 1], :], preferred_element_type=F32)
            at = (which, *idx)
            scores[at] = scores[at] + value.reshape(SIDE, SIDE, own_rows, features)

    steps = [gather.steps(p) for p in range(PARTS)]
    early = [
        [functools.partial(give, p), functools.partial(take, p), *steps[p][:3]] for p in range(PARTS)
    ]
    for turn in range(len(early[0]) + PARTS - 1):
        for p in reversed(range(PARTS)):
            if 0 <= turn - p < len(early[p]):
                early[p][turn - p]()
    for p in range(PARTS):
        encode(p, 0)
    for i in range(3):
        for p in range(PARTS):
            steps[p][3][i]()
    for p in range(PARTS):
        encode(p, -1)
        encode(p, 1)
    for p in range(PARTS):
        steps[p][4]()
        encode(p, 2)

    def rectify(delta):
        idx = torus.index(0, (None, None, delta))
        for which in range(2):
            feats[(which, *idx)] = jnp.maximum(scores[(which, *idx)], 0.0).astype(BF16)

    own_out = pltpu.make_async_copy(feats.at[core], feat_hbm.at[:, :, :, core], feat_sem)
    cross_out = remote(
        feats.at[other], feat_hbm.at[:, :, :, core], cross_send.at[3], cross_recv.at[3], partner
    )
    cross_in = remote(
        feats.at[other], feat_hbm.at[:, :, :, other], cross_send.at[3], cross_recv.at[3], partner
    )

    scatter = Scatter(torus, total, planes, lines, blocks, rs_send, rs_recv)

    def produce(p, delta):
        if (p, delta) == (0, 2):
            rectify(2)
        if (p, delta) == (1, 2):
            for d in (0, 1, -1):
                rectify(d)
            own_out.start()
            cross_out.start()
        idx = torus.index(p, (None, None, delta))
        value = 0.0
        for which in range(2):
            block = feats[(which, *idx)].reshape(SIDE * SIDE * own_rows, features)
            value = value + jnp.dot(
                block, dec[which, :, p * width : (p + 1) * width], preferred_element_type=F32
            )
        total[(p, *idx)] = value.astype(BF16).reshape(SIDE, SIDE, own_rows, width)

    def finish(p, value):
        rec_ref[:, p * width : (p + 1) * width] = value

    scatter.run(produce, finish)

    own_out.wait()
    cross_out.wait_send()
    cross_in.wait_recv()
    for copy in sent:
        copy.wait_send()
    gather.drain()
    scatter.drain()


def layer(tokens, ids, weights, routed, shared, encoder, encoder_bias, decoder):
    n_e, n_f = lax.axis_size("expert"), lax.axis_size("feat")
    own_rows = ids.shape[1]
    model = tokens.shape[1]
    hid = routed[0].shape[2]
    slots = n_e * own_rows
    rows = n_f * own_rows
    features = encoder.shape[1]
    width = model // PARTS
    cube = (SIDE, SIDE, SIDE)
    vmem = pl.BlockSpec(memory_space=pltpu.VMEM)
    hbm = pl.BlockSpec(memory_space=pl.ANY)
    dma = pltpu.SemaphoreType.DMA
    plane_rows = pltpu.VMEM((n_e, own_rows, model), BF16)
    torus_sem = dma((PARTS, COPIES))
    return pl.pallas_call(
        layer_kernel,
        name="layer",
        out_shape=(
            jax.ShapeDtypeStruct((*cube, 2, own_rows, features), BF16),
            jax.ShapeDtypeStruct((own_rows, model), F32),
        ),
        in_specs=[hbm] * 12,
        out_specs=(hbm, vmem),
        scratch_shapes=[pltpu.VMEM(w.shape[1:], BF16) for w in routed]
        + [pltpu.VMEM(w.shape, BF16) for w in shared]
        + [
            pltpu.VMEM((2 * TOP, rows), F32),
            pltpu.VMEM((n_f, 2 * TOP, rows), F32),
            pltpu.VMEM((n_f, own_rows, model), F32),
            pltpu.VMEM((2, rows, slots), BF16),
            plane_rows,
            plane_rows,
            pltpu.VMEM((2, HALF * own_rows, hid), BF16),
            plane_rows,
            plane_rows,
            pltpu.VMEM((n_f, own_rows, model), BF16),
            pltpu.VMEM((n_f - 1, own_rows, model), BF16),
            *(pltpu.VMEM((*cube, own_rows, SPLIT[p + 1] - SPLIT[p]), BF16) for p in range(PARTS)),
            pltpu.VMEM((PARTS, *cube, own_rows, width), BF16),
            pltpu.VMEM((PARTS, 3, SIDE, SIDE, own_rows, width), BF16),
            pltpu.VMEM((PARTS, 3, SIDE, own_rows, width), BF16),
            pltpu.VMEM((PARTS, 3, own_rows, width), BF16),
            pltpu.VMEM((2, *cube, own_rows, features), F32),
            pltpu.VMEM((2, *cube, own_rows, features), BF16),
            pltpu.VMEM((2, model, features), BF16),
            pltpu.VMEM((2, features, model), BF16),
            pltpu.VMEM((2, 1, features), F32),
            pltpu.VMEM(tokens.shape, BF16),
            pltpu.VMEM(ids.shape, ids.dtype),
            pltpu.VMEM(weights.shape, weights.dtype),
            dma((13,)),
            dma((n_f - 1,)),
            dma((n_f - 1,)),
            dma((n_e - 1,)),
            dma((n_e - 1,)),
            dma((PARTS, n_e - 1)),
            dma((PARTS, n_e - 1)),
            dma((PARTS, n_f - 1)),
            dma((PARTS, n_f - 1)),
            torus_sem, torus_sem, torus_sem, torus_sem,
            dma((4,)),
            dma((4,)),
        ],
        compiler_params=pltpu.CompilerParams(
            collective_id=0, has_side_effects=True, vmem_limit_bytes=63 * 1024 * 1024
        ),
    )(tokens, ids, weights, *routed, *shared, encoder, encoder_bias, decoder)


def finish_kernel(feat_hbm, sums_hbm, bias_hbm, out_hbm, rec_hbm, held, sums, bias, in_sem, out_sem):
    reads = [
        pltpu.make_async_copy(sums_hbm, sums, in_sem.at[SIDE]),
        pltpu.make_async_copy(bias_hbm, bias, in_sem.at[SIDE + 1]),
    ] + [pltpu.make_async_copy(feat_hbm.at[y], held.at[y], in_sem.at[y]) for y in range(SIDE)]
    writes = [pltpu.make_async_copy(sums, rec_hbm, out_sem.at[SIDE])] + [
        pltpu.make_async_copy(held.at[y], out_hbm.at[y], out_sem.at[y]) for y in range(SIDE)
    ]
    for copy in reads:
        copy.start()
    reads[0].wait()
    reads[1].wait()
    lanes = bias.shape[1]
    for i in range(bias.shape[0]):
        cols = slice(i * lanes, (i + 1) * lanes)
        sums[:, cols] = sums[:, cols] + bias[i : i + 1, :]
    for y in range(SIDE):
        reads[2 + y].wait()
        writes[1 + y].start()
    writes[0].start()
    for copy in writes:
        copy.wait()


def finish(features, sums, bias):
    hbm = pl.BlockSpec(memory_space=pl.ANY)
    bias = bias.reshape(-1, 128)
    return pl.pallas_call(
        finish_kernel,
        name="finish",
        out_shape=(
            jax.ShapeDtypeStruct(features.shape, features.dtype),
            jax.ShapeDtypeStruct(sums.shape, sums.dtype),
        ),
        in_specs=[hbm] * 3,
        out_specs=(hbm, hbm),
        scratch_shapes=[
            pltpu.VMEM(features.shape, features.dtype),
            pltpu.VMEM(sums.shape, sums.dtype),
            pltpu.VMEM(bias.shape, bias.dtype),
            pltpu.SemaphoreType.DMA((SIDE + 2,)),
            pltpu.SemaphoreType.DMA((SIDE + 1,)),
        ],
        compiler_params=pltpu.CompilerParams(vmem_limit_bytes=60 * 1024 * 1024),
    )(features, sums, bias)


def shards(
    tokens,
    expert_ids,
    gate_weights,
    expert_gate,
    expert_up,
    expert_down,
    shared_gate,
    shared_up,
    shared_down,
    encoder,
    encoder_bias,
    decoder,
    decoder_bias,
):
    features, sums = layer(
        tokens,
        expert_ids.T,
        gate_weights.T,
        (expert_gate, expert_up, expert_down),
        (shared_gate, shared_up, shared_down),
        encoder,
        encoder_bias[None, :],
        decoder,
    )
    features, sums = finish(features, sums, decoder_bias)
    return features.reshape(-1, encoder.shape[1]), sums


def solution(mesh):
    return jax.shard_map(
        shards,
        mesh=mesh,
        in_specs=(
            P("expert", None),
            P(("expert", "feat"), None),
            P(("expert", "feat"), None),
            P(("expert", "feat"), None, None),
            P(("expert", "feat"), None, None),
            P(("expert", "feat"), None, None),
            P(None, "feat"),
            P(None, "feat"),
            P("feat", None),
            P(None, ("expert", "feat")),
            P(("expert", "feat")),
            P(("expert", "feat"), None),
            P(),
        ),
        out_specs=(P(None, ("expert", "feat")), P(("expert", "feat"), None)),
        check_vma=False,
    )
```
